128 devices in a mesh: dp: 32 (over x, y_lo, z), segment: 4 (over y_hi, core).
Axes of the slice: x: 4, y: 4 (y_hi: 2, y_lo: 2; y = y_hi * 2 + y_lo), z: 4, core: 2. Of those that a mesh axis runs over, the one named last changes fastest.
Arguments:
- query_cache: bfloat16 [1024, 4096], P(('dp', 'segment')), may hold values from -0.125 to 0.125, as said below
- passage_cache: bfloat16 [1024, 4096], P(('dp', 'segment')), may hold values from -0.125 to 0.125, as said below
- hard_offsets: int32 [1024, 1], P(('dp', 'segment')), may hold values from 0 to 127
- passage_lengths: int32 [8], replicated, may hold values from 1 to 256, 512 in all
- segment_inputs: bfloat16 [4, 512, 4096], P('segment', 'dp'), may hold values from -6 to 6
- segment_cotangents: bfloat16 [4, 512, 4096], P('segment', 'dp'), may hold values from -6 to 6
- norm_gain: float32 [4, 4096], P('segment'), may hold values from 0.5 to 1.5
- gate_weight: bfloat16 [4, 4096, 14336], P('segment', None, 'dp'), may hold values from -0.09375 to 0.09375
- up_weight: bfloat16 [4, 4096, 14336], P('segment', None, 'dp'), may hold values from -0.09375 to 0.09375
- down_weight: bfloat16 [4, 14336, 4096], P('segment', 'dp'), may hold values from -0.046875 to 0.046875
Outputs:
- query_grads: bfloat16 [1024, 4096], P(('dp', 'segment'))
- passage_grads: bfloat16 [1024, 4096], P(('dp', 'segment'))
- input_grads: bfloat16 [4, 512, 4096], P('segment', 'dp')
- gate_grads: bfloat16 [4, 4096, 14336], P('segment', None, 'dp')
- up_grads: bfloat16 [4, 4096, 14336], P('segment', None, 'dp')
- down_grads: bfloat16 [4, 14336, 4096], P('segment', 'dp')
- gain_grads: float32 [4, 4096], P('segment')
The draws below stay inside these ranges and needn't reach their ends.
Inputs may be any that keep to these rules, and one draw needn't show every extreme that they name: Query i's hard negative k is passage (i // 128) * 128 + hard_offsets[i, k]. `passage_lengths`: the lengths sum to 512; the longest is exactly 256. `query_cache`: cached query embeddings, no row zero. `passage_cache`: cached passage embeddings, no row zero.
All inputs are finite; a program needn't handle non-finite values.
Results may differ from the reference program's by a relative error of at most 0.0071.
Values may be sent and summed in bfloat16 or wider, within the bound.
A program may use at most 128 MiB of HBM per device.

```python
import math
import jax
import jax.numpy as jnp
import numpy as np
from jax import lax

D = 4096
FF = 14336
PAIR_DEV = 8
NEG = 1
HN_BLOCK = 128
PAIRS = 1024
SEGMENT_TOK = 512
MB_PASS = 8
N_SEGMENT = 4


def shared_parts(key):
    base_key = jax.random.fold_in(key, 4711)
    topic_key = jax.random.fold_in(base_key, 1)
    label_key = jax.random.fold_in(base_key, 2)
    noise_key = jax.random.fold_in(base_key, 3)
    topics = jax.random.normal(topic_key, (8, D), jnp.float32)
    labels = jax.random.randint(label_key, (PAIRS,), 0, 8)
    common = jax.random.normal(noise_key, (PAIRS, D), jnp.float32)
    strength = 0.7
    return (jnp.take(topics, labels, axis=0) * strength, common)


def own_noise_rows(key):
    return jax.random.normal(key, (PAIRS, D), jnp.float32)


def finish_rows(key, row_values):
    scaled = row_values / math.sqrt(D)
    clip_bound = 8.0 / math.sqrt(D)
    return jnp.clip(scaled, -clip_bound, clip_bound).astype(jnp.bfloat16)


def draw_query_cache(key, part):
    topic_rows, common = shared_parts(key)
    return finish_rows(jax.random.fold_in(key, 11), topic_rows + common)


def draw_passage_cache(key, part):
    topic_rows, common = shared_parts(key)
    own_noise = own_noise_rows(jax.random.fold_in(key, 12))
    return finish_rows(jax.random.fold_in(key, 13), topic_rows + 0.05 * common + own_noise)


def plant(values, rng, least, high):
    extent = values.shape
    index_at = [jax.random.randint(jax.random.fold_in(rng, axis), (), 0, extent[axis]) for axis in range(len(extent))]
    values = values.at[tuple(index_at)].set(least)
    longest = extent.index(max(extent))
    index_at[longest] = (index_at[longest] + 1) % extent[longest]
    return values.at[tuple(index_at)].set(high)


def levels(stream_key, shape, cuts, smallest, largest):
    def one(axis_at, parts):
        steps = jax.random.uniform(jax.random.fold_in(jax.random.fold_in(stream_key, 6), axis_at), (parts,), jnp.float32, smallest / len(cuts), largest / len(cuts))
        return jnp.repeat(jnp.exp(steps), shape[axis_at] // parts).reshape((-1,) + (1,) * (len(shape) - axis_at - 1))

    loudness = one(*cuts[0])
    for cut in cuts[1:]:
        loudness = loudness * one(*cut)
    return loudness


def length_profile(count, total, limit, lean):
    loads = [(1 << 20) // math.isqrt(standing ** lean) + 1 for standing in range(2, count + 1)]
    spare, holding = total - limit - (count - 1), [1] * (count - 1)
    while spare > 0:
        free = [i for i in range(count - 1) if holding[i] < limit]
        pool, left = sum([loads[i] for i in free]), spare
        for i in free:
            more = min(limit - holding[i], max(1, left * loads[i] // pool), spare)
            holding[i] = holding[i] + more
            spare = spare - more
    return np.array([limit] + holding)


def ragged(key, number_of, total, limit, slope):
    if number_of == 2:
        one = jax.random.randint(key, (), max(1, total - limit), min(limit, total - 1) + 1)
        return jnp.stack([one, total - one])
    sizes = jnp.asarray(length_profile(number_of, total, limit, slope), jnp.int32)
    couples = (number_of - 1) // 2
    giver, taker = sizes[1:1 + 2 * couples:2], sizes[2:2 + 2 * couples:2]
    margin = jnp.minimum(giver - 1, limit - taker)
    shifted = jax.random.randint(jax.random.fold_in(key, 1), (couples,), 0, 1 << 20) % (margin + 1)
    sizes = sizes.at[1:1 + 2 * couples:2].set(giver - shifted).at[2:2 + 2 * couples:2].set(taker + shifted)
    return sizes[jax.random.permutation(jax.random.fold_in(key, 2), number_of)]


def bell_draw(stream_key, shape, scale, bound, pieces=(), kind=jnp.bfloat16):
    result = scale * jax.random.normal(stream_key, shape, jnp.float32)
    if pieces:
        result = result * levels(stream_key, shape, pieces, -0.22, 0.18)
    return jnp.clip(result, -bound, bound).astype(kind)


def setup_inputs(seed: int = 0) -> dict:
    keys = jax.random.split(jax.random.key(seed), 11)
    return {
        "query_cache": draw_query_cache(jax.random.fold_in(keys[10], 71), 0),
        "passage_cache": draw_passage_cache(jax.random.fold_in(keys[10], 71), 0),
        "hard_offsets": plant(jax.random.randint(keys[2], (PAIRS, NEG), 0, HN_BLOCK), jax.random.fold_in(keys[2], 1), 0, HN_BLOCK - 1).astype(jnp.int32),
        "passage_lengths": ragged(keys[3], MB_PASS, SEGMENT_TOK, SEGMENT_TOK // 2, 2).astype(jnp.int32),
        "segment_inputs": bell_draw(keys[4], (N_SEGMENT, SEGMENT_TOK, D), 1.0, 6.0, ((0, 4), (1, 32))),
        "segment_cotangents": bell_draw(keys[5], (N_SEGMENT, SEGMENT_TOK, D), 1.0, 6.0, ((0, 4), (1, 32))),
        "norm_gain": jnp.clip(1.0 + 0.1 * jax.random.normal(keys[6], (N_SEGMENT, D), jnp.float32), 0.5, 1.5),
        "gate_weight": bell_draw(keys[7], (N_SEGMENT, D, FF), D ** -0.5, 0.09375, ((0, 4), (2, 32))),
        "up_weight": bell_draw(keys[8], (N_SEGMENT, D, FF), D ** -0.5, 0.09375, ((0, 4), (2, 32))),
        "down_weight": bell_draw(keys[9], (N_SEGMENT, FF, D), FF ** -0.5, 0.046875, ((0, 4), (1, 32))),
    }


TAU = 0.02
HN_WEIGHT = 64.0
EPS_NORM = 1e-06
EPS_RMS = 1e-05

def unit_rows(values):
    widened = values.astype(jnp.float32)
    inverse = lax.rsqrt(lax.optimization_barrier(jnp.sum(widened * widened, axis=-1, keepdims=True)) + EPS_NORM)
    return (widened * inverse, inverse)

def unit_back(gradient, unit_value, inverse):
    return inverse * (gradient - unit_value * lax.optimization_barrier(jnp.sum(gradient * unit_value, axis=-1, keepdims=True)))

def hard_weights(hard_offsets, first_row, column_index):
    row_index = first_row + jnp.arange(hard_offsets.shape[0], dtype=jnp.int32)
    picked = row_index // HN_BLOCK * HN_BLOCK
    picked = picked[:, None] + hard_offsets
    tallies = jnp.zeros((hard_offsets.shape[0], column_index.shape[0]), jnp.float32)
    for column in range(hard_offsets.shape[1]):
        tallies = tallies + (picked[:, column:column + 1] == column_index[None, :]).astype(jnp.float32)
    return 1.0 + HN_WEIGHT * tallies

def mean_pool_back(passage_lengths, token_index, rows):
    last_tokens = jnp.cumsum(passage_lengths).astype(jnp.int32) - 1
    first_tokens = last_tokens - passage_lengths + 1
    member = (token_index[:, None] >= first_tokens[None, :]) & (token_index[:, None] <= last_tokens[None, :])
    selector = member.astype(jnp.float32) / passage_lengths.astype(jnp.float32)[None, :]
    return jnp.dot(selector, rows.astype(jnp.float32), precision=lax.Precision.HIGHEST).astype(jnp.bfloat16)

def layer_grads(inputs, cotangent, gain_row, gate_matrix, up_matrix, down_matrix):
    widened = inputs.astype(jnp.float32)
    inverse = lax.rsqrt(lax.optimization_barrier(jnp.mean(widened * widened, axis=-1, keepdims=True)) + EPS_RMS)
    unit_value = widened * inverse
    normed = (unit_value * gain_row).astype(jnp.bfloat16)
    gate_value = jnp.dot(normed, gate_matrix, preferred_element_type=jnp.float32)
    up_value = jnp.dot(normed, up_matrix, preferred_element_type=jnp.float32)
    sigmoid_gate = jax.nn.sigmoid(gate_value)
    activation = gate_value * sigmoid_gate
    hidden = (activation * up_value).astype(jnp.bfloat16)
    hidden_delta = jnp.dot(cotangent, down_matrix.T, preferred_element_type=jnp.float32)
    up_delta = (hidden_delta * activation).astype(jnp.bfloat16)
    gate_delta = (hidden_delta * up_value * sigmoid_gate * (1.0 + gate_value * (1.0 - sigmoid_gate))).astype(jnp.bfloat16)
    down_grad = jnp.dot(hidden.T, cotangent, preferred_element_type=jnp.float32).astype(jnp.bfloat16)
    gate_grad = jnp.dot(normed.T, gate_delta, preferred_element_type=jnp.float32).astype(jnp.bfloat16)
    up_grad = jnp.dot(normed.T, up_delta, preferred_element_type=jnp.float32).astype(jnp.bfloat16)
    normed_delta = jnp.dot(gate_delta, gate_matrix.T, preferred_element_type=jnp.float32) + jnp.dot(up_delta, up_matrix.T, preferred_element_type=jnp.float32)
    gain_grad = lax.optimization_barrier(jnp.sum(normed_delta * unit_value, axis=0))
    scaled_delta = normed_delta * gain_row
    input_grad = cotangent.astype(jnp.float32) + inverse * (scaled_delta - unit_value * lax.optimization_barrier(jnp.mean(scaled_delta * unit_value, axis=-1, keepdims=True)))
    return (input_grad.astype(jnp.bfloat16), gate_grad, up_grad, down_grad, gain_grad)

def reference(query_cache, passage_cache, hard_offsets, passage_lengths, segment_inputs, segment_cotangents, norm_gain, gate_weight, up_weight, down_weight):
    query_unit, query_inverse = unit_rows(query_cache)
    passage_unit, passage_inverse = unit_rows(passage_cache)
    query_low = query_unit.astype(jnp.bfloat16)
    passage_low = passage_unit.astype(jnp.bfloat16)
    scores = jnp.dot(query_low, passage_low.T, preferred_element_type=jnp.float32) / TAU
    column_index = jnp.arange(PAIRS, dtype=jnp.int32)
    weights = hard_weights(hard_offsets, 0, column_index)
    weighted = weights * jnp.exp(scores)
    totals = lax.optimization_barrier(jnp.sum(weighted, axis=1, keepdims=True))
    positive = (column_index[:, None] == column_index[None, :]).astype(jnp.float32)
    dscore = (weighted / totals - positive).astype(jnp.bfloat16)
    query_dir = jnp.dot(dscore, passage_low, preferred_element_type=jnp.float32) / TAU
    passage_dir = jnp.dot(dscore.T, query_low, preferred_element_type=jnp.float32) / TAU
    query_grads = unit_back(query_dir, query_unit, query_inverse).astype(jnp.bfloat16)
    passage_grads = unit_back(passage_dir, passage_unit, passage_inverse).astype(jnp.bfloat16)
    first_pass = (N_SEGMENT - 1) * PAIR_DEV
    batch_rows = passage_grads[first_pass:first_pass + MB_PASS]
    token_index = jnp.arange(SEGMENT_TOK, dtype=jnp.int32)
    pooled = mean_pool_back(passage_lengths, token_index, batch_rows)
    results = []
    for section in range(N_SEGMENT):
        if section < N_SEGMENT - 1:
            cotangent = segment_cotangents[section]
        else:
            cotangent = pooled
        results.append(layer_grads(segment_inputs[section], cotangent, norm_gain[section], gate_weight[section], up_weight[section], down_weight[section]))
    input_grads = jnp.stack([item[0] for item in results])
    gate_grads = jnp.stack([item[1] for item in results])
    up_grads = jnp.stack([item[2] for item in results])
    down_grads = jnp.stack([item[3] for item in results])
    gain_grads = jnp.stack([item[4] for item in results])
    return (query_grads, passage_grads, input_grads, gate_grads, up_grads, down_grads, gain_grads)
```

```python
import functools

import jax
import jax.numpy as jnp
from jax import lax
from jax.experimental import pallas as pl
from jax.experimental.pallas import tpu as pltpu
from jax.sharding import PartitionSpec as P

HN_BLOCK = 128
TAU = 0.02
HN_WEIGHT = 64.0
EPS_NORM = 1e-06
EPS_RMS = 1e-05

D = 4096
ROWS = 8
TOK = 16
NX, NY, NZ = 4, 2, 4
NA, NB = 8, 16
H = D // 2
Q = D // 4
VMEM_LIMIT = 46 * 1024 * 1024
F32 = jnp.float32
BF16 = jnp.bfloat16
MESH = pl.DeviceIdType.MESH


class Place:
    def __init__(self):
        dp = lax.axis_index("dp")
        segment = lax.axis_index("segment")
        self.x = dp // 8
        self.y = lax.rem(dp // 4, 2)
        self.z = lax.rem(dp, 4)
        self.y_hi = segment // 2
        self.core = lax.rem(segment, 2)
        self.segment = segment

    def section(self, x=None, y=None, z=None):
        x = self.x if x is None else x
        y = self.y if y is None else y
        z = self.z if z is None else z
        return {"dp": x * 8 + y * 4 + z, "segment": self.segment}

    def shift(self, axis, by):
        at = getattr(self, axis)
        return lax.rem(at + by, 4)

    def a_index(self):
        return self.x * 2 + self.core

    def b_index(self):
        return (self.y_hi * 2 + self.y) * 4 + self.z

    def a_device(self, index):
        return {
            "dp": (index // 2) * 8 + self.y * 4 + self.z,
            "segment": self.y_hi * 2 + lax.rem(index, 2),
        }

    def b_device(self, index):
        y_all = index // 4
        return {
            "dp": self.x * 8 + lax.rem(y_all, 2) * 4 + lax.rem(index, 4),
            "segment": (y_all // 2) * 2 + self.core,
        }


def remote(src, dst, send_sem, recv_sem, device):
    return pltpu.make_async_remote_copy(
        src_ref=src, dst_ref=dst, send_sem=send_sem, recv_sem=recv_sem, device_id=device, device_id_type=MESH
    )


class Gather:
    COPIES = 25

    def __init__(self, place, src, buf, send_sem, recv_sem, local_sem):
        self.p, self.buf = place, buf
        self.send_sem, self.recv_sem = send_sem, recv_sem
        slot = buf.at[place.x, place.y, place.z]
        self.local = pltpu.make_async_copy(src, slot, local_sem)
        self.copies = {}
        self.add("y", src, slot, place.section(y=1 - place.y))
        for tag, axis, stage, base in (("a", "x", 0, 0), ("b", "z", 0, 2), ("c", "z", 1, 0), ("d", "x", 1, 2)):
            at = getattr(place, axis)
            left, right = place.shift(axis, 3), place.shift(axis, 1)
            plus, minus = place.section(**{axis: right}), place.section(**{axis: left})
            moves = (
                (at, base, plus),
                (at, base + 1, minus),
                (at, base + 1, plus),
                (at, base, minus),
                (left, base, plus),
                (right, base + 1, minus),
            )
            for k, (block, quarter, device) in enumerate(moves):
                view = self.view(axis, stage, block, quarter)
                self.add((tag, k), view, view, device)

    def add(self, key, src, dst, device):
        i = len(self.copies)
        self.copies[key] = remote(src, dst, self.send_sem.at[i], self.recv_sem.at[i], device)

    def view(self, axis, stage, at, quarter):
        p, c = self.p, pl.ds(quarter * Q, Q)
        if axis == "x":
            return self.buf.at[at, :, p.z, :, c] if stage == 0 else self.buf.at[at, :, :, :, c]
        return self.buf.at[p.x, :, at, :, c] if stage == 0 else self.buf.at[:, :, at, :, c]

    def begin(self, *keys):
        for key in keys:
            self.copies[key].start()

    def got(self, *keys):
        for key in keys:
            self.copies[key].wait_recv()

    def pair(self):
        self.local.start()
        self.begin("y")

    def small(self):
        self.local.wait()
        self.got("y")
        for k in range(4):
            self.begin(("a", k), ("b", k))

    def relay(self, one, two):
        for tag in (one, two):
            self.got((tag, 0))
            self.begin((tag, 4))
        for tag in (one, two):
            self.got((tag, 1))
            self.begin((tag, 5))

    def large_first(self):
        for tag in ("a", "b"):
            self.got(*[(tag, k) for k in (2, 3, 4, 5)])
        self.begin(("c", 0), ("d", 0), ("c", 1), ("d", 1))

    def large_second(self):
        self.begin(("c", 2), ("d", 2), ("c", 3), ("d", 3))

    def arrive(self):
        for tag in ("c", "d"):
            self.got(*[(tag, k) for k in (2, 3, 4, 5)])

    def sent(self):
        for copy in self.copies.values():
            copy.wait_send()


def unit_rows(values, eps, mean):
    widened = values.astype(F32)
    total = jnp.sum(widened * widened, axis=-1, keepdims=True)
    if mean:
        total = total / D
    inverse = lax.rsqrt(total + eps)
    return widened * inverse, inverse


def unit_back(gradient, unit_value, inverse):
    return inverse * (gradient - unit_value * jnp.sum(gradient * unit_value, axis=-1, keepdims=True))


def rows_at(index, rows=ROWS):
    return pl.ds(pl.multiple_of(index * rows, rows), rows)


class Links:
    def __init__(self, send_sem, recv_sem):
        self.send_sem, self.recv_sem = send_sem, recv_sem
        self.copies = []

    def send(self, src, dst, device):
        i = len(self.copies)
        copy = remote(src, dst, self.send_sem.at[i], self.recv_sem.at[i], device)
        copy.start()
        self.copies.append(copy)
        return copy

    def finish(self):
        for copy in self.copies:
            copy.wait_send()


class RingSum:
    def __init__(self, place, links, axis, part, far, near, out):
        self.p, self.links, self.axis = place, links, axis
        self.part, self.far, self.near, self.out = part, far, near, out
        self.plus = place.section(**{axis: place.shift(axis, 1)})
        self.minus = place.section(**{axis: place.shift(axis, 3)})
        self.at = [place.shift(axis, k) for k in range(4)]

    def start(self, q):
        send = self.links.send
        if q == 0:
            self.f0 = send(self.part(self.at[2], 0), self.far.at[0], self.plus)
            self.n10 = send(self.part(self.at[3], 0), self.near.at[1, 0], self.minus)
        else:
            self.f1 = send(self.part(self.at[2], 1), self.far.at[1], self.minus)
            self.n01 = send(self.part(self.at[1], 1), self.near.at[0, 1], self.plus)

    def relay(self):
        send = self.links.send
        self.f0.wait_recv()
        add_into(self.far.at[0], self.part(self.at[1], 0))
        self.n00 = send(self.far.at[0], self.near.at[0, 0], self.plus)
        self.f1.wait_recv()
        add_into(self.far.at[1], self.part(self.at[3], 1))
        self.n11 = send(self.far.at[1], self.near.at[1, 1], self.minus)

    def end(self):
        for copy, other, q in ((self.n10, self.n00, 0), (self.n01, self.n11, 1)):
            copy.wait_recv()
            other.wait_recv()
            add_three(self.out(q), self.part(self.at[0], q), self.near.at[0, q], self.near.at[1, q])


def lead_loop(ref, body):
    shape = ref.shape
    lead = shape[:-2]
    count = 1
    for n in lead:
        count *= n

    @pl.loop(0, count)
    def _(i):
        index = []
        for n in reversed(lead):
            index.append(lax.rem(i, n))
            i = i // n
        body(tuple(reversed(index)))


def add_into(target, term):
    def body(i):
        target[i] = (target[i].astype(F32) + term[i].astype(F32)).astype(BF16)

    lead_loop(target, body)


def add_three(out, one, two, three):
    def body(i):
        out[i] = (one[i].astype(F32) + (two[i].astype(F32) + three[i].astype(F32))).astype(BF16)

    lead_loop(out, body)


TOKENS = NX * NY * NZ * TOK
SPAN = TOKENS // 2
CHUNK = 512
DEPTH = 1024
FF_HERE = 448
FF_STEP = 64
RING_COPIES = 26


def step_kernel(*refs):
    names = [n for n, _ in INPUTS] + [n for n, _ in OUTPUTS] + [n for n, _ in scratch()]
    r = dict(zip(names, refs, strict=True))
    place = Place()
    a, b = place.a_index(), place.b_index()
    y_all = place.y_hi * 2 + place.y
    a_at = [lax.rem(a + k, NA) for k in range(NA)]
    a_dev = [place.a_device(i) for i in a_at]
    z_at = [place.shift("z", k) for k in range(NZ)]
    ya_at = [lax.rem(y_all + k, 4) for k in range(4)]
    z_dev = [place.section(z=z) for z in z_at]
    x_dev = [place.section(x=place.shift("x", k)) for k in range(NX)]
    ya_dev = [place.b_device(y * 4 + place.z) for y in ya_at]
    y_dev = place.section(y=1 - place.y)
    is_last = place.segment == 3
    not_last = jnp.logical_not(is_last)

    barrier = pltpu.get_barrier_semaphore()
    for device in a_dev[1:] + z_dev[1:] + ya_dev[1:]:
        pl.semaphore_signal(barrier, inc=1, device_id=device, device_id_type=MESH)

    loads = [
        pltpu.make_async_copy(r[src], r[dst], r["load_sem"].at[i])
        for i, (src, dst) in enumerate((("gate_hbm", "gate_w"), ("up_hbm", "up_w"), ("down_hbm", "down_w")))
    ]
    for copy in loads:
        copy.start()

    p_unit, _ = unit_rows(r["passage"][...], EPS_NORM, False)
    r["p_all"][rows_at(b), :] = p_unit.astype(BF16)
    q_unit, _ = unit_rows(r["query"][...], EPS_NORM, False)
    r["q_all"][rows_at(a), :] = q_unit.astype(BF16)
    normed, _ = unit_rows(r["inputs"][...], EPS_RMS, True)
    r["normed_own"][...] = (normed * r["gain"][...]).astype(BF16)
    lane = lax.broadcasted_iota(jnp.int32, (ROWS, ROWS), 1)
    diagonal = lane == lax.broadcasted_iota(jnp.int32, (ROWS, ROWS), 0)
    spread = jnp.broadcast_to(r["offsets"][...].astype(F32), (ROWS, ROWS))
    column = jnp.sum(jnp.where(diagonal, spread, 0.0), axis=1, keepdims=True)
    r["off_all"][a] = jnp.broadcast_to(column, (ROWS, 128)).astype(jnp.int32)

    pl.semaphore_wait(barrier, NA + 5)

    def fan(devices, view_of, name):
        copies = []
        for k in range(1, len(devices)):
            src, dst = view_of(k)
            copy = remote(src, dst, r[name + "_send"].at[k], r[name + "_recv"].at[k], devices[k])
            copy.start()
            copies.append(copy)
        return copies

    normed_all, cot_all = r["normed_all"], r["cot_all"]
    g0 = Gather(place, r["normed_own"], normed_all, r["g_send"].at[0], r["g_recv"].at[0], r["g_local"].at[0])
    g1 = Gather(place, r["cotangent"], cot_all, r["g_send"].at[1], r["g_recv"].at[1], r["g_local"].at[1])

    own_p = r["p_all"].at[rows_at(b)]
    own_q = r["q_all"].at[rows_at(a)]
    pz = fan(z_dev, lambda k: (own_p, own_p), "pz")
    g0.pair()
    qs = fan(a_dev, lambda k: (own_q, own_q), "q")
    os = fan(a_dev, lambda k: (r["off_all"].at[a], r["off_all"].at[a]), "o")
    pl.when(not_last)(g1.pair)
    for copy in pz:
        copy.wait_recv()
    group = r["p_all"].at[rows_at(y_all, 32)]
    py = fan(ya_dev, lambda k: (group, group), "py")
    g0.small()
    pl.when(not_last)(g1.small)
    g0.relay("a", "b")
    pl.when(not_last)(lambda: g1.relay("a", "b"))
    g0.large_first()

    for copy in qs + os + py:
        copy.wait_recv()
    scores = (
        lax.dot_general(r["q_all"][...], r["p_all"][...], (((1,), (1,)), ((), ())), preferred_element_type=F32)
        / TAU
    )
    row = lax.broadcasted_iota(jnp.int32, (NA * ROWS, NB * ROWS), 0)
    col = lax.broadcasted_iota(jnp.int32, (NA * ROWS, NB * ROWS), 1)
    row_a, col_b = row >> 3, col >> 3
    row_dev = ((row_a >> 1) * 8 + place.y * 4 + place.z) * 4 + place.y_hi * 2 + (row_a & 1)
    row_index = row_dev * ROWS + (row & 7)
    col_y = col_b >> 2
    col_dev = (place.x * 8 + (col_y & 1) * 4 + (col_b & 3)) * 4 + (col_y >> 1) * 2 + place.core
    col_index = col_dev * ROWS + (col & 7)
    offsets = r["off_all"][...].reshape(NA * ROWS, 128)
    picked = (row_index >> 7) * HN_BLOCK + offsets
    weights = 1.0 + HN_WEIGHT * (picked == col_index).astype(F32)
    weighted = weights * jnp.exp(scores)
    part = jnp.sum(weighted, axis=1, keepdims=True)
    tot_all = r["tot_all"]
    tot_all[a] = jnp.broadcast_to(part, (NA * ROWS, 128))
    ts = fan(a_dev, lambda k: (tot_all.at[a], tot_all.at[a]), "t")
    g0.large_second()

    for copy in ts:
        copy.wait_recv()
    totals = tot_all[0]
    for k in range(1, NA):
        totals = totals + tot_all[k]
    positive = (row_index == col_index).astype(F32)
    dscore = weighted / totals - positive
    dscore_low = dscore.astype(BF16)
    dscore_t = dscore.T.astype(BF16)

    def direction(left, right, own, low):
        @pl.loop(0, D // CHUNK)
        def _(c):
            cols = pl.ds(pl.multiple_of(c * CHUNK, CHUNK), CHUNK)
            value = jnp.dot(left, right[:, cols], preferred_element_type=F32) / TAU
            own[:, cols] = value
            low[:, cols] = value.astype(BF16)

    pd_own, pd_low, pd_y, pd_z = r["pd_own"], r["pd_low"], r["pd_y"], r["pd_z"]
    direction(dscore_t, r["q_all"], pd_own, pd_low)
    pdy = fan(ya_dev, lambda k: (pd_low.at[rows_at(ya_at[k], 32)], pd_y.at[k - 1]), "pdy")
    g0.relay("c", "d")
    direction(dscore_low, r["p_all"], r["qd_own"], r["qd_low"])
    pl.when(not_last)(g1.large_first)

    for copy in pdy:
        copy.wait_recv()
    mine = rows_at(y_all, 32)

    @pl.loop(0, D // CHUNK)
    def _(c):
        cols = pl.ds(pl.multiple_of(c * CHUNK, CHUNK), CHUNK)
        value = pd_own[mine, cols]
        for k in range(3):
            value = value + pd_y[k, :, cols].astype(F32)
        pd_own[mine, cols] = value
        pd_low[mine, cols] = value.astype(BF16)

    pdz = fan(z_dev, lambda k: (pd_low.at[rows_at(y_all * 4 + z_at[k])], pd_z.at[k - 1]), "pdz")
    pl.when(not_last)(g1.large_second)

    g0.arrive()
    for copy in loads:
        copy.wait()

    def tokens_of(buf, half, at):
        return buf[2 * half : 2 * half + 2, :, :, :, at].reshape(SPAN, DEPTH)

    def contract(weight, buf, out, half, first):
        cols = pl.ds(first, SPAN)

        def one(i):
            at = pl.ds(pl.multiple_of(i * DEPTH, DEPTH), DEPTH)
            return lax.dot_general(
                weight[:, at], tokens_of(buf, half, at), (((1,), (1,)), ((), ())), preferred_element_type=F32
            )

        out[:, cols] = one(0)

        @pl.loop(1, D // DEPTH)
        def _(i):
            out[:, cols] += one(i)

    contract(r["gate_w"], normed_all, r["gate_t"], 0, 0)

    for copy in pdz:
        copy.wait_recv()
    passage_dir = pd_own[rows_at(b), :]
    for k in range(3):
        passage_dir = passage_dir + pd_z[k].astype(F32)
    p_unit, p_inverse = unit_rows(r["passage"][...], EPS_NORM, False)
    passage_grads = unit_back(passage_dir, p_unit, p_inverse).astype(BF16)
    r["passage_grads"][...] = passage_grads

    batch_buf = r["batch_buf"]
    at_root = is_last & (place.x == 0) & (place.y == 0) & (place.z == 0)
    on_column = is_last & (place.x == 0) & (place.y == 0)

    def tree(i, device):
        return remote(batch_buf, batch_buf, r["b_send"].at[i], r["b_recv"].at[i], device)

    z_copies = [tree(k - 1, z_dev[k]) for k in range(1, NZ)]
    x_copies = [tree(2 + k, x_dev[k]) for k in range(1, NX)]
    y_copy = tree(6, y_dev)

    @pl.when(at_root)
    def _():
        batch_buf[...] = passage_grads
        for copy in z_copies:
            copy.start()

    pl.when(not_last)(lambda: g1.relay("c", "d"))
    qds = fan(a_dev, lambda k: (r["qd_low"].at[rows_at(a_at[k])], r["qd_land"].at[k - 1]), "qd")
    contract(r["gate_w"], normed_all, r["gate_t"], 1, SPAN)

    for k in range(1, NZ):
        pl.when(on_column & (place.z == k))(z_copies[k - 1].wait_recv)

    @pl.when(on_column)
    def _():
        for copy in x_copies:
            copy.start()

    contract(r["up_w"], normed_all, r["up_t"], 0, 0)

    for k in range(1, NX):
        pl.when(is_last & (place.x == k) & (place.y == 0))(x_copies[k - 1].wait_recv)
    pl.when(is_last & (place.y == 0))(y_copy.start)
    contract(r["up_w"], normed_all, r["up_t"], 1, SPAN)
    pl.when(is_last & (place.y == 1))(y_copy.wait_recv)
    pl.when(not_last)(g1.arrive)

    @pl.when(is_last)
    def _():
        token = lax.broadcasted_iota(jnp.int32, (TOKENS, 128), 0)
        slot = lax.broadcasted_iota(jnp.int32, (TOKENS, 128), 1)
        which = lax.broadcasted_iota(jnp.int32, (ROWS, 128), 0)
        member = jnp.zeros((TOKENS, 128), F32)
        count = jnp.zeros((ROWS, 128), F32)
        first = 0
        for m in range(ROWS):
            length = r["lengths"][m]
            last = first + length - 1
            hit = (slot == m) & (token >= first) & (token <= last)
            member = member + jnp.where(hit, 1.0, 0.0)
            count = count + jnp.where(which == m, length, 0).astype(F32)
            first = first + length
        member = member.astype(BF16)
        share = (1.0 / count)[:, :1]

        @pl.loop(0, D // CHUNK)
        def _(c):
            cols = pl.ds(pl.multiple_of(c * CHUNK, CHUNK), CHUNK)
            scaled = batch_buf[:, cols].astype(F32) * share
            padded = jnp.concatenate([scaled, jnp.zeros((128 - ROWS, CHUNK), F32)], axis=0).astype(BF16)
            pooled = jnp.dot(member, padded, preferred_element_type=F32).astype(BF16)
            cot_all[:, :, :, :, cols] = pooled.reshape(NX, NY, NZ, TOK, CHUNK)

    hidden_t, gate_d, up_d = r["hidden_t"], r["gate_d"], r["up_d"]
    for half in range(2):
        contract(r["down_w"], cot_all, r["delta_t"], half, 0)

        @pl.loop(0, FF_HERE // FF_STEP)
        def _(i, half=half):
            rows = pl.ds(pl.multiple_of(i * FF_STEP, FF_STEP), FF_STEP)
            cols = pl.ds(half * SPAN, SPAN)
            gate, up, delta = r["gate_t"][rows, cols], r["up_t"][rows, cols], r["delta_t"][rows, :]
            sigmoid = jax.nn.sigmoid(gate)
            activation = gate * sigmoid
            hidden_t[rows, cols] = (activation * up).astype(BF16)
            up_d[rows, cols] = (delta * activation).astype(BF16)
            gate_d[rows, cols] = (delta * up * sigmoid * (1.0 + gate * (1.0 - sigmoid))).astype(BF16)

        here = pl.ds(half * SPAN, SPAN)
        r["gate_rows"][here, :] = gate_d[:, here].T
        r["up_rows"][here, :] = up_d[:, here].T

    links = Links(r["ring_send"], r["ring_recv"])
    gain_links = Links(r["gain_send"], r["gain_recv"])
    part_all, gain_y, gain_x, gain_z = r["part_all"], r["gain_y"], r["gain_x"], r["gain_z"]

    def cols_of(q):
        return pl.ds(q * Q, Q)

    def partial(quarter):
        @pl.loop(0, Q // CHUNK)
        def _(i):
            at = pl.ds(pl.multiple_of(quarter * Q + i * CHUNK, CHUNK), CHUNK)
            delta = jnp.dot(r["gate_rows"][...], r["gate_w"][:, at], preferred_element_type=F32)
            delta = delta + jnp.dot(r["up_rows"][...], r["up_w"][:, at], preferred_element_type=F32)
            tokens = normed_all[:, :, :, :, at].reshape(TOKENS, CHUNK).astype(F32)
            gain_y[place.y, :, at] = jnp.sum(delta * tokens, axis=0, keepdims=True)
            part_all[:, :, :, :, at] = delta.astype(BF16).reshape(NX, NY, NZ, TOK, CHUNK)

    def weight_grad(out_ref, rows_ref, buf, first, last):
        @pl.loop(first, last)
        def _(i):
            at = pl.ds(pl.multiple_of(i * CHUNK, CHUNK), CHUNK)
            tokens = buf[:, :, :, :, at].reshape(TOKENS, CHUNK)
            out_ref[:, at] = jnp.dot(rows_ref[...], tokens, preferred_element_type=F32).astype(BF16)

    def stored(i, buf, out):
        copy = pltpu.make_async_copy(r[buf], r[out], r["store_sem"].at[i])
        copy.start()
        return copy

    first0 = RingSum(
        place,
        links,
        "z",
        lambda at, q: part_all.at[:, :, at, :, cols_of(q)],
        r["far_z0"],
        r["near_z0"],
        lambda q: r["sum0"].at[:, :, :, cols_of(q)],
    )
    first1 = RingSum(
        place,
        links,
        "x",
        lambda at, q: part_all.at[at, :, :, :, cols_of(2 + q)],
        r["far_x1"],
        r["near_x1"],
        lambda q: r["sum1"].at[:, :, :, cols_of(q)],
    )
    second0 = RingSum(
        place,
        links,
        "x",
        lambda at, q: r["sum0"].at[at, :, :, cols_of(q)],
        r["far_x0"],
        r["near_x0"],
        lambda q: r["two0"].at[:, :, cols_of(q)],
    )
    second1 = RingSum(
        place,
        links,
        "z",
        lambda at, q: r["sum1"].at[:, at, :, cols_of(q)],
        r["far_z1"],
        r["near_z1"],
        lambda q: r["two1"].at[:, :, cols_of(q)],
    )

    partial(0)
    first0.start(0)
    partial(2)
    first1.start(0)
    partial(1)
    first0.start(1)
    partial(3)
    first1.start(1)
    gain_copy = gain_links.send(gain_y.at[place.y], gain_y.at[place.y], y_dev)
    weight_grad(r["gate_w"], gate_d, normed_all, 0, 6)
    first0.relay()
    first1.relay()
    weight_grad(r["gate_w"], gate_d, normed_all, 6, 8)
    stores = [stored(0, "gate_w", "gate_grads")]
    gain_copy.wait_recv()
    gain_x[place.x] = gain_y[0] + gain_y[1]
    gain_copies = [gain_links.send(gain_x.at[place.x], gain_x.at[place.x], d) for d in x_dev[1:]]
    weight_grad(r["up_w"], up_d, normed_all, 0, 8)
    stores.append(stored(1, "up_w", "up_grads"))

    for copy in qds:
        copy.wait_recv()
    query_dir = r["qd_own"][rows_at(a), :]
    for k in range(NA - 1):
        query_dir = query_dir + r["qd_land"][k].astype(F32)
    q_unit, q_inverse = unit_rows(r["query"][...], EPS_NORM, False)
    r["query_grads"][...] = unit_back(query_dir, q_unit, q_inverse).astype(BF16)

    first0.end()
    second0.start(0)
    second0.start(1)
    first1.end()
    second1.start(0)
    second1.start(1)
    for copy in gain_copies:
        copy.wait_recv()
    gain_z[place.z] = (gain_x[0] + gain_x[1]) + (gain_x[2] + gain_x[3])
    gain_copies = [gain_links.send(gain_z.at[place.z], gain_z.at[place.z], d) for d in z_dev[1:]]
    weight_grad(r["down_w"], hidden_t, cot_all, 0, 4)
    second0.relay()
    second1.relay()
    weight_grad(r["down_w"], hidden_t, cot_all, 4, 8)
    stores.append(stored(2, "down_w", "down_grads"))
    two0, two1, y_recv = r["two0"], r["two1"], r["y_recv"]
    second0.end()
    y0 = links.send(two0.at[1 - place.y], y_recv.at[0], y_dev)
    second1.end()
    y1 = links.send(two1.at[1 - place.y], y_recv.at[1], y_dev)
    unit, inverse = unit_rows(r["inputs"][...], EPS_RMS, True)
    for copy in gain_copies:
        copy.wait_recv()
    r["gain_grads"][...] = ((gain_z[0] + gain_z[1]) + (gain_z[2] + gain_z[3])) / r["gain"][...]

    y0.wait_recv()
    y1.wait_recv()
    delta = jnp.concatenate(
        [
            two0[place.y].astype(F32) + y_recv[0].astype(F32),
            two1[place.y].astype(F32) + y_recv[1].astype(F32),
        ],
        axis=1,
    )
    scaled = delta * r["gain"][...]
    mean = jnp.sum(scaled * unit, axis=-1, keepdims=True) / D
    own_cot = cot_all[place.x, place.y, place.z].astype(F32)
    r["input_grads"][...] = (own_cot + inverse * (scaled - unit * mean)).astype(BF16)

    for copy in stores:
        copy.wait()
    g0.sent()
    pl.when(not_last)(g1.sent)
    for copy in pz + py + qs + os + ts + pdy + pdz + qds:
        copy.wait_send()

    @pl.when(at_root)
    def _():
        for copy in z_copies:
            copy.wait_send()

    @pl.when(on_column)
    def _():
        for copy in x_copies:
            copy.wait_send()

    pl.when(is_last & (place.y == 0))(y_copy.wait_send)
    links.finish()
    gain_links.finish()


ANY, VMEM, SMEM = pl.ANY, pltpu.VMEM, pltpu.SMEM
INPUTS = (
    ("query", VMEM),
    ("passage", VMEM),
    ("offsets", VMEM),
    ("lengths", SMEM),
    ("inputs", VMEM),
    ("cotangent", VMEM),
    ("gain", VMEM),
    ("gate_hbm", ANY),
    ("up_hbm", ANY),
    ("down_hbm", ANY),
)
OUTPUTS = (
    ("query_grads", ((ROWS, D), BF16, VMEM)),
    ("passage_grads", ((ROWS, D), BF16, VMEM)),
    ("input_grads", ((TOK, D), BF16, VMEM)),
    ("gain_grads", ((1, D), F32, VMEM)),
    ("gate_grads", ((FF_HERE, D), BF16, ANY)),
    ("up_grads", ((FF_HERE, D), BF16, ANY)),
    ("down_grads", ((FF_HERE, D), BF16, ANY)),
)


def scratch():
    dma = pltpu.SemaphoreType.DMA
    every = pltpu.VMEM((NX, NY, NZ, TOK, D), BF16)
    weight = pltpu.VMEM((FF_HERE, D), BF16)
    wide = pltpu.VMEM((FF_HERE, TOKENS), F32)
    low = pltpu.VMEM((FF_HERE, TOKENS), BF16)
    tall = pltpu.VMEM((TOKENS, FF_HERE), BF16)
    items = [
        ("normed_own", pltpu.VMEM((TOK, D), BF16)),
        ("normed_all", every),
        ("cot_all", every),
        ("part_all", every),
        ("gate_w", weight),
        ("up_w", weight),
        ("down_w", weight),
        ("gate_t", wide),
        ("up_t", wide),
        ("delta_t", pltpu.VMEM((FF_HERE, SPAN), F32)),
        ("hidden_t", low),
        ("gate_d", low),
        ("up_d", low),
        ("gate_rows", tall),
        ("up_rows", tall),
        ("q_all", pltpu.VMEM((NA * ROWS, D), BF16)),
        ("p_all", pltpu.VMEM((NB * ROWS, D), BF16)),
        ("off_all", pltpu.VMEM((NA, ROWS, 128), jnp.int32)),
        ("tot_all", pltpu.VMEM((NA, NA * ROWS, 128), F32)),
        ("qd_own", pltpu.VMEM((NA * ROWS, D), F32)),
        ("qd_low", pltpu.VMEM((NA * ROWS, D), BF16)),
        ("qd_land", pltpu.VMEM((NA - 1, ROWS, D), BF16)),
        ("pd_own", pltpu.VMEM((NB * ROWS, D), F32)),
        ("pd_low", pltpu.VMEM((NB * ROWS, D), BF16)),
        ("pd_y", pltpu.VMEM((3, 32, D), BF16)),
        ("pd_z", pltpu.VMEM((3, ROWS, D), BF16)),
        ("batch_buf", pltpu.VMEM((ROWS, D), BF16)),
        ("far_z0", pltpu.VMEM((2, NX, NY, TOK, Q), BF16)),
        ("near_z0", pltpu.VMEM((2, 2, NX, NY, TOK, Q), BF16)),
        ("far_x0", pltpu.VMEM((2, NY, TOK, Q), BF16)),
        ("near_x0", pltpu.VMEM((2, 2, NY, TOK, Q), BF16)),
        ("far_x1", pltpu.VMEM((2, NY, NZ, TOK, Q), BF16)),
        ("near_x1", pltpu.VMEM((2, 2, NY, NZ, TOK, Q), BF16)),
        ("far_z1", pltpu.VMEM((2, NY, TOK, Q), BF16)),
        ("near_z1", pltpu.VMEM((2, 2, NY, TOK, Q), BF16)),
        ("sum0", pltpu.VMEM((NX, NY, TOK, H), BF16)),
        ("sum1", pltpu.VMEM((NY, NZ, TOK, H), BF16)),
        ("two0", pltpu.VMEM((NY, TOK, H), BF16)),
        ("two1", pltpu.VMEM((NY, TOK, H), BF16)),
        ("y_recv", pltpu.VMEM((2, TOK, H), BF16)),
        ("gain_y", pltpu.VMEM((2, 1, D), F32)),
        ("gain_x", pltpu.VMEM((4, 1, D), F32)),
        ("gain_z", pltpu.VMEM((4, 1, D), F32)),
        ("load_sem", dma((3,))),
        ("store_sem", dma((3,))),
        ("g_send", dma((2, Gather.COPIES))),
        ("g_recv", dma((2, Gather.COPIES))),
        ("g_local", dma((2,))),
        ("b_send", dma((7,))),
        ("b_recv", dma((7,))),
        ("ring_send", dma((RING_COPIES,))),
        ("ring_recv", dma((RING_COPIES,))),
        ("gain_send", dma((7,))),
        ("gain_recv", dma((7,))),
    ]
    for name, count in (("pz", 4), ("py", 4), ("q", NA), ("o", NA), ("t", NA), ("pdy", 4), ("pdz", 4), ("qd", NA)):
        items += [(name + "_send", dma((count,))), (name + "_recv", dma((count,)))]
    return items


def local(
    query_cache,
    passage_cache,
    hard_offsets,
    passage_lengths,
    segment_inputs,
    segment_cotangents,
    norm_gain,
    gate_weight,
    up_weight,
    down_weight,
):
    results = pl.pallas_call(
        step_kernel,
        out_shape=[jax.ShapeDtypeStruct(shape, kind) for _, (shape, kind, _) in OUTPUTS],
        in_specs=[pl.BlockSpec(memory_space=space) for _, space in INPUTS],
        out_specs=[pl.BlockSpec(memory_space=space) for _, (_, _, space) in OUTPUTS],
        scratch_shapes=[item for _, item in scratch()],
        compiler_params=pltpu.CompilerParams(
            collective_id=0, has_side_effects=True, vmem_limit_bytes=VMEM_LIMIT
        ),
        name="step",
    )(
        query_cache,
        passage_cache,
        hard_offsets.reshape(1, ROWS),
        passage_lengths,
        segment_inputs[0],
        segment_cotangents[0],
        norm_gain,
        gate_weight[0].T,
        up_weight[0].T,
        down_weight[0],
    )
    query_grads, passage_grads, input_grads, gain_grads, gate_grads, up_grads, down_grads = results
    return (
        query_grads,
        passage_grads,
        input_grads[None],
        gate_grads.T[None],
        up_grads.T[None],
        down_grads[None],
        gain_grads,
    )


def solution(mesh):
    placed = (
        P(("dp", "segment"), None),
        P(("dp", "segment"), None),
        P(("dp", "segment"), None),
        P(),
        P("segment", "dp", None),
        P("segment", "dp", None),
        P("segment", None),
        P("segment", None, "dp"),
        P("segment", None, "dp"),
        P("segment", "dp", None),
    )
    return jax.shard_map(
        local,
        mesh=mesh,
        in_specs=placed,
        out_specs=(
            P(("dp", "segment"), None),
            P(("dp", "segment"), None),
            P("segment", "dp", None),
            P("segment", None, "dp"),
            P("segment", None, "dp"),
            P("segment", "dp", None),
            P("segment", None),
        ),
        check_vma=False,
    )
```

```python
import functools

import jax
import jax.numpy as jnp
from jax import lax
from jax.experimental import pallas as pl
from jax.experimental.pallas import tpu as pltpu
from jax.sharding import PartitionSpec as P

HN_BLOCK = 128
TAU = 0.02
PER_TAU = 1.0 / TAU
HN_WEIGHT = 64.0
EPS_NORM = 1e-06
EPS_RMS = 1e-05

D = 4096
ROWS = 8
TOK = 16
NX, NY, NZ = 4, 2, 4
NA, NB = 8, 16
H = D // 2
Q = D // 4
VMEM_LIMIT = 45 * 1024 * 1024
F32 = jnp.float32
BF16 = jnp.bfloat16
MESH = pl.DeviceIdType.MESH


class Place:
    def __init__(self):
        dp = lax.axis_index("dp")
        segment = lax.axis_index("segment")
        self.x = dp // 8
        self.y = lax.rem(dp // 4, 2)
        self.z = lax.rem(dp, 4)
        self.y_hi = segment // 2
        self.core = lax.rem(segment, 2)
        self.segment = segment

    def section(self, x=None, y=None, z=None):
        x = self.x if x is None else x
        y = self.y if y is None else y
        z = self.z if z is None else z
        return {"dp": x * 8 + y * 4 + z, "segment": self.segment}

    def shift(self, axis, by):
        at = getattr(self, axis)
        return lax.rem(at + by, 4)

    def a_index(self):
        return self.x * 2 + self.core

    def b_index(self):
        return (self.y_hi * 2 + self.y) * 4 + self.z

    def a_device(self, index):
        return {
            "dp": (index // 2) * 8 + self.y * 4 + self.z,
            "segment": self.y_hi * 2 + lax.rem(index, 2),
        }

    def b_device(self, index):
        y_all = index // 4
        return {
            "dp": self.x * 8 + lax.rem(y_all, 2) * 4 + lax.rem(index, 4),
            "segment": (y_all // 2) * 2 + self.core,
        }


def remote(src, dst, send_sem, recv_sem, device):
    return pltpu.make_async_remote_copy(
        src_ref=src, dst_ref=dst, send_sem=send_sem, recv_sem=recv_sem, device_id=device, device_id_type=MESH
    )


class Gather:
    COPIES = 25

    def __init__(self, place, src, buf, send_sem, recv_sem, local_sem):
        self.p, self.buf = place, buf
        self.send_sem, self.recv_sem = send_sem, recv_sem
        slot = buf.at[place.x, place.y, place.z]
        self.local = pltpu.make_async_copy(src, slot, local_sem)
        self.copies = {}
        self.add("y", src, slot, place.section(y=1 - place.y))
        for tag, axis, stage, base in (("a", "x", 0, 0), ("b", "z", 0, 2), ("c", "z", 1, 0), ("d", "x", 1, 2)):
            at = getattr(place, axis)
            left, right = place.shift(axis, 3), place.shift(axis, 1)
            plus, minus = place.section(**{axis: right}), place.section(**{axis: left})
            moves = (
                (at, base, plus),
                (at, base + 1, minus),
                (at, base + 1, plus),
                (at, base, minus),
                (left, base, plus),
                (right, base + 1, minus),
            )
            for k, (block, quarter, device) in enumerate(moves):
                view = self.view(axis, stage, block, quarter)
                self.add((tag, k), view, view, device)

    def add(self, key, src, dst, device):
        i = len(self.copies)
        self.copies[key] = remote(src, dst, self.send_sem.at[i], self.recv_sem.at[i], device)

    def view(self, axis, stage, at, quarter):
        p, c = self.p, pl.ds(quarter * Q, Q)
        if axis == "x":
            return self.buf.at[at, :, p.z, :, c] if stage == 0 else self.buf.at[at, :, :, :, c]
        return self.buf.at[p.x, :, at, :, c] if stage == 0 else self.buf.at[:, :, at, :, c]

    def begin(self, *keys):
        for key in keys:
            self.copies[key].start()

    def got(self, *keys):
        for key in keys:
            self.copies[key].wait_recv()

    def pair(self):
        self.local.start()
        self.begin("y")

    def small(self):
        self.local.wait()
        self.got("y")
        for k in range(4):
            self.begin(("a", k), ("b", k))

    def relay(self, one, two):
        for tag in (one, two):
            self.got((tag, 0))
            self.begin((tag, 4))
        for tag in (one, two):
            self.got((tag, 1))
            self.begin((tag, 5))

    def large_first(self):
        for tag in ("a", "b"):
            self.got(*[(tag, k) for k in (2, 3, 4, 5)])
        self.begin(("c", 0), ("d", 0), ("c", 1), ("d", 1))

    def large_second(self):
        self.begin(("c", 2), ("d", 2), ("c", 3), ("d", 3))

    def arrive(self):
        for tag in ("c", "d"):
            self.got(*[(tag, k) for k in (2, 3, 4, 5)])

    def sent(self):
        for copy in self.copies.values():
            copy.wait_send()


def unit_rows(values, eps, mean):
    widened = values.astype(F32)
    total = jnp.sum(widened * widened, axis=-1, keepdims=True)
    if mean:
        total = total / D
    inverse = lax.rsqrt(total + eps)
    return widened * inverse, inverse


def unit_back(gradient, unit_value, inverse):
    return inverse * (gradient - unit_value * jnp.sum(gradient * unit_value, axis=-1, keepdims=True))


def rows_at(index, rows=ROWS):
    return pl.ds(pl.multiple_of(index * rows, rows), rows)


class Links:
    def __init__(self, send_sem, recv_sem):
        self.send_sem, self.recv_sem = send_sem, recv_sem
        self.copies = []

    def send(self, src, dst, device):
        i = len(self.copies)
        copy = remote(src, dst, self.send_sem.at[i], self.recv_sem.at[i], device)
        copy.start()
        self.copies.append(copy)
        return copy

    def finish(self):
        for copy in self.copies:
            copy.wait_send()


class RingSum:
    def __init__(self, place, links, axis, part, far, near, out):
        self.p, self.links, self.axis = place, links, axis
        self.part, self.far, self.near, self.out = part, far, near, out
        self.plus = place.section(**{axis: place.shift(axis, 1)})
        self.minus = place.section(**{axis: place.shift(axis, 3)})
        self.at = [place.shift(axis, k) for k in range(4)]

    def start(self, q):
        send = self.links.send
        if q == 0:
            self.f0 = send(self.part(self.at[2], 0), self.far.at[0], self.plus)
            self.n10 = send(self.part(self.at[3], 0), self.near.at[1, 0], self.minus)
        else:
            self.f1 = send(self.part(self.at[2], 1), self.far.at[1], self.minus)
            self.n01 = send(self.part(self.at[1], 1), self.near.at[0, 1], self.plus)

    def relay(self, q):
        send = self.links.send
        if q == 0:
            self.f0.wait_recv()
            add_into(self.far.at[0], self.part(self.at[1], 0))
            self.n00 = send(self.far.at[0], self.near.at[0, 0], self.plus)
        else:
            self.f1.wait_recv()
            add_into(self.far.at[1], self.part(self.at[3], 1))
            self.n11 = send(self.far.at[1], self.near.at[1, 1], self.minus)

    def end(self, q):
        for copy in (self.n10, self.n00) if q == 0 else (self.n01, self.n11):
            copy.wait_recv()
        add_three(self.out(q), self.part(self.at[0], q), self.near.at[0, q], self.near.at[1, q])


def lead_loop(ref, body):
    shape = ref.shape
    lead = shape[:-2]
    count = 1
    for n in lead:
        count *= n

    @pl.loop(0, count)
    def _(i):
        index = []
        for n in reversed(lead):
            index.append(lax.rem(i, n))
            i = i // n
        body(tuple(reversed(index)))


def add_into(target, term):
    def body(i):
        target[i] = (target[i].astype(F32) + term[i].astype(F32)).astype(BF16)

    lead_loop(target, body)


def add_three(out, one, two, three):
    def body(i):
        out[i] = (one[i].astype(F32) + (two[i].astype(F32) + three[i].astype(F32))).astype(BF16)

    lead_loop(out, body)


TOKENS = NX * NY * NZ * TOK
SPAN = TOKENS // 2
CHUNK = 512
DEPTH = 1024
FF_HERE = 448
FF_STEP = 64
RING_COPIES = 26


def step_kernel(*refs):
    names = [n for n, _ in INPUTS] + [n for n, _, _ in OUTPUTS] + [n for n, _ in scratch()]
    r = dict(zip(names, refs, strict=True))
    place = Place()
    a, b = place.a_index(), place.b_index()
    y_all = place.y_hi * 2 + place.y
    a_at = [lax.rem(a + k, NA) for k in range(NA)]
    a_dev = [place.a_device(i) for i in a_at]
    z_at = [place.shift("z", k) for k in range(NZ)]
    ya_at = [lax.rem(y_all + k, 4) for k in range(4)]
    z_dev = [place.section(z=z) for z in z_at]
    x_dev = [place.section(x=place.shift("x", k)) for k in range(NX)]
    ya_dev = [place.b_device(y * 4 + place.z) for y in ya_at]
    y_dev = place.section(y=1 - place.y)
    is_last = place.segment == 3
    not_last = jnp.logical_not(is_last)

    barrier = pltpu.get_barrier_semaphore()
    for device in a_dev[1:] + z_dev[1:] + ya_dev[1:]:
        pl.semaphore_signal(barrier, inc=1, device_id=device, device_id_type=MESH)

    loads = {
        name: pltpu.make_async_copy(r[name + "_hbm"], r[name], r["load_sem"].at[i]) for i, name in enumerate(LOADED)
    }
    for copy in loads.values():
        copy.start()
    packed = r["packed"]
    r["query"] = packed.at[0:8]
    r["passage"] = packed.at[8:16]
    r["inputs"] = packed.at[16:32]
    r["cotangent"] = packed.at[32:48]

    def row_to_column(values):
        return jnp.sum(jnp.where(diagonal, jnp.broadcast_to(values, (ROWS, ROWS)), 0.0), axis=1, keepdims=True)

    lane = lax.broadcasted_iota(jnp.int32, (ROWS, ROWS), 1)
    diagonal = lane == lax.broadcasted_iota(jnp.int32, (ROWS, ROWS), 0)

    p_unit, _ = unit_rows(r["passage"][...], EPS_NORM, False)
    r["p_all"][rows_at(b), :] = p_unit.astype(BF16)
    q_unit, _ = unit_rows(r["query"][...], EPS_NORM, False)
    r["q_all"][rows_at(a), :] = q_unit.astype(BF16)
    normed, _ = unit_rows(r["inputs"][...], EPS_RMS, True)
    r["normed_own"][...] = (normed * r["gain"][...]).astype(BF16)
    column = row_to_column(r["small"][:, 0:8].astype(F32))
    r["off_all"][a] = jnp.broadcast_to(column, (ROWS, 128)).astype(jnp.int32)

    pl.semaphore_wait(barrier, NA + 5)

    def fan(devices, view_of, name):
        copies = []
        for k in range(1, len(devices)):
            src, dst = view_of(k)
            copy = remote(src, dst, r[name + "_send"].at[k], r[name + "_recv"].at[k], devices[k])
            copy.start()
            copies.append(copy)
        return copies

    normed_all, cot_all = r["normed_all"], r["cot_all"]
    g0 = Gather(place, r["normed_own"], normed_all, r["g_send"].at[0], r["g_recv"].at[0], r["g_local"].at[0])
    g1 = Gather(place, r["cotangent"], cot_all, r["g_send"].at[1], r["g_recv"].at[1], r["g_local"].at[1])

    own_p = r["p_all"].at[rows_at(b)]
    own_q = r["q_all"].at[rows_at(a)]
    def group(y, half):
        return r["p_all"].at[rows_at(y, 32), pl.ds(half * H, H)]

    y_moves = (
        (ya_at[0], 0, ya_dev[1]),
        (ya_at[0], 1, ya_dev[3]),
        (ya_at[0], 1, ya_dev[1]),
        (ya_at[0], 0, ya_dev[3]),
        (ya_at[3], 0, ya_dev[1]),
        (ya_at[1], 1, ya_dev[3]),
    )
    py = [
        remote(group(y, half), group(y, half), r["py_send"].at[k], r["py_recv"].at[k], device)
        for k, (y, half, device) in enumerate(y_moves)
    ]
    pz = fan(z_dev, lambda k: (own_p, own_p), "pz")
    g0.pair()
    pl.when(not_last)(g1.pair)
    for copy in pz:
        copy.wait_recv()
    for copy in py[:4]:
        copy.start()
    g0.small()
    qs = fan(a_dev, lambda k: (own_q, own_q), "q")
    os = fan(a_dev, lambda k: (r["off_all"].at[a], r["off_all"].at[a]), "o")
    pl.when(not_last)(g1.small)
    py[0].wait_recv()
    py[4].start()
    py[1].wait_recv()
    py[5].start()
    g0.relay("a", "b")
    pl.when(not_last)(lambda: g1.relay("a", "b"))
    g0.large_first()
    g0.large_second()

    for copy in qs + os + py[2:]:
        copy.wait_recv()
    scores = (
        lax.dot_general(r["q_all"][...], r["p_all"][...], (((1,), (1,)), ((), ())), preferred_element_type=F32)
        * PER_TAU
    )
    row = lax.broadcasted_iota(jnp.int32, (NA * ROWS, NB * ROWS), 0)
    col = lax.broadcasted_iota(jnp.int32, (NA * ROWS, NB * ROWS), 1)
    row_a, col_b = row >> 3, col >> 3
    row_dev = ((row_a >> 1) * 8 + place.y * 4 + place.z) * 4 + place.y_hi * 2 + (row_a & 1)
    row_index = row_dev * ROWS + (row & 7)
    col_y = col_b >> 2
    col_dev = (place.x * 8 + (col_y & 1) * 4 + (col_b & 3)) * 4 + (col_y >> 1) * 2 + place.core
    col_index = col_dev * ROWS + (col & 7)
    offsets = r["off_all"][...].reshape(NA * ROWS, 128)
    picked = (row_index >> 7) * HN_BLOCK + offsets
    weights = 1.0 + HN_WEIGHT * (picked == col_index).astype(F32)
    weighted = weights * jnp.exp(scores)
    part = jnp.sum(weighted, axis=1, keepdims=True)
    tot_all = r["tot_all"]
    on_row = col == row
    tot_all[a] = jnp.broadcast_to(jnp.sum(jnp.where(on_row, part, 0.0), axis=0, keepdims=True), (ROWS, 128))
    ts = fan(a_dev, lambda k: (tot_all.at[a], tot_all.at[a]), "t")
    g0.relay("c", "d")
    pl.when(not_last)(g1.large_first)

    for copy in ts:
        copy.wait_recv()
    totals = tot_all[0]
    for k in range(1, NA):
        totals = totals + tot_all[k]
    totals = jnp.broadcast_to(totals[:1, :], (NA * ROWS, 128))
    totals = jnp.sum(jnp.where(on_row, totals, 0.0), axis=1, keepdims=True)
    positive = (row_index == col_index).astype(F32)
    dscore = weighted / totals - positive
    dscore_low = dscore.astype(BF16)
    dscore_t = dscore.T.astype(BF16)

    def direction(left, right, own, low):
        @pl.loop(0, D // CHUNK)
        def _(c):
            cols = pl.ds(pl.multiple_of(c * CHUNK, CHUNK), CHUNK)
            value = jnp.dot(left, right[:, cols], preferred_element_type=F32) * PER_TAU
            own[:, cols] = value
            low[:, cols] = value.astype(BF16)

    pd_own, pd_low, pd_y, pd_z = r["pd_own"], r["pd_low"], r["pd_y"], r["pd_z"]
    direction(dscore_t, r["q_all"], pd_own, pd_low)
    head = pl.ds(0, ROWS)
    rest = pl.ds(ROWS, 3 * ROWS)

    def rest_of(y):
        return pl.ds(pl.multiple_of(y * 32 + ROWS, ROWS), 3 * ROWS)

    pdy = fan(ya_dev, lambda k: (pd_low.at[rows_at(ya_at[k] * 4)], pd_y.at[k - 1, head]), "pdy")
    pdr = fan(ya_dev, lambda k: (pd_low.at[rest_of(ya_at[k])], pd_y.at[k - 1, rest]), "pdr")
    direction(dscore_low, r["p_all"], r["qd_own"], r["qd_low"])
    pl.when(not_last)(g1.large_second)

    def gathered_rows(rows, local_rows, step):
        @pl.loop(0, D // step)
        def _(c):
            cols = pl.ds(pl.multiple_of(c * step, step), step)
            value = pd_own[rows, cols]
            for k in range(3):
                value = value + pd_y[k, local_rows, cols].astype(F32)
            pd_own[rows, cols] = value
            pd_low[rows, cols] = value.astype(BF16)

    for copy in pdy:
        copy.wait_recv()
    first_rows = rows_at(y_all * 4)
    gathered_rows(first_rows, head, 2 * DEPTH)
    root_dev = place.section(z=0)
    to_root = [
        remote(pd_low.at[first_rows], pd_z.at[k - 1], r["root_send"].at[k], r["root_recv"].at[k], root_dev)
        for k in range(1, NZ)
    ]
    for k in range(1, NZ):
        pl.when(place.z == k)(to_root[k - 1].start)
    pl.when(not_last)(lambda: g1.relay("c", "d"))

    g0.arrive()
    for name in ("gate_w", "up_w", "down_w"):
        loads[name].wait()

    def tokens_of(buf, half, at):
        return buf[2 * half : 2 * half + 2, :, :, :, at].reshape(SPAN, DEPTH)

    def contract(weight, buf, out, half, first):
        cols = pl.ds(first, SPAN)

        def one(i):
            at = pl.ds(pl.multiple_of(i * DEPTH, DEPTH), DEPTH)
            return lax.dot_general(
                weight[:, at], tokens_of(buf, half, at), (((1,), (1,)), ((), ())), preferred_element_type=F32
            )

        out[:, cols] = one(0)

        @pl.loop(1, D // DEPTH)
        def _(i):
            out[:, cols] += one(i)

    contract(r["gate_w"], normed_all, r["gate_t"], 0, 0)

    def passage_end():
        passage_dir = pd_own[rows_at(b), :]
        for k in range(3):
            passage_dir = passage_dir + pd_z[k].astype(F32)
        unit, inverse = unit_rows(r["passage"][...], EPS_NORM, False)
        r["passage_grads"][...] = unit_back(passage_dir, unit, inverse).astype(BF16)

    @pl.when(place.z == 0)
    def _():
        for copy in to_root:
            copy.wait_recv()
        passage_end()

    batch_buf = r["batch_buf"]
    at_root = is_last & (place.x == 0) & (place.y == 0) & (place.z == 0)
    on_column = is_last & (place.x == 0) & (place.y == 0)

    def tree(i, device):
        return remote(batch_buf, batch_buf, r["b_send"].at[i], r["b_recv"].at[i], device)

    z_copies = [tree(k - 1, z_dev[k]) for k in range(1, NZ)]
    x_copies = [tree(2 + k, x_dev[k]) for k in range(1, NX)]
    y_copy = tree(6, y_dev)

    @pl.when(at_root)
    def _():
        batch_buf[...] = r["passage_grads"][...]
        for copy in z_copies:
            copy.start()

    contract(r["gate_w"], normed_all, r["gate_t"], 1, SPAN)

    for k in range(1, NZ):
        pl.when(on_column & (place.z == k))(z_copies[k - 1].wait_recv)

    @pl.when(on_column)
    def _():
        for copy in x_copies:
            copy.start()

    contract(r["up_w"], normed_all, r["up_t"], 0, 0)

    for k in range(1, NX):
        pl.when(is_last & (place.x == k) & (place.y == 0))(x_copies[k - 1].wait_recv)
    pl.when(is_last & (place.y == 0))(y_copy.start)
    contract(r["up_w"], normed_all, r["up_t"], 1, SPAN)
    qds = fan(a_dev, lambda k: (r["qd_low"].at[rows_at(a_at[k])], r["qd_land"].at[k - 1]), "qd")
    for copy in pdr:
        copy.wait_recv()
    gathered_rows(rest_of(y_all), rest, CHUNK)
    pdz = [
        remote(
            pd_low.at[rows_at(y_all * 4 + z_at[k])],
            pd_z.at[k - 1],
            r["pdz_send"].at[k],
            r["pdz_recv"].at[k],
            z_dev[k],
        )
        for k in range(1, NZ)
    ]
    for k in range(1, NZ):
        pl.when(z_at[k] != 0)(pdz[k - 1].start)
    pl.when(is_last & (place.y == 1))(y_copy.wait_recv)
    pl.when(not_last)(g1.arrive)

    @pl.when(is_last)
    def _():
        length = row_to_column(r["small"][:, 8:16].astype(F32))
        upto = jnp.where(lane >= lax.broadcasted_iota(jnp.int32, (ROWS, ROWS), 0), length, 0.0)
        last = jnp.sum(upto, axis=0, keepdims=True).astype(jnp.int32) - 1
        first = last - r["small"][:, 8:16] + 1
        last = jnp.concatenate([last, jnp.full((1, 128 - ROWS), -1, jnp.int32)], axis=1)
        first = jnp.concatenate([first, jnp.zeros((1, 128 - ROWS), jnp.int32)], axis=1)
        token = lax.broadcasted_iota(jnp.int32, (TOKENS, 128), 0)
        member = jnp.where((token >= first) & (token <= last), 1.0, 0.0).astype(BF16)
        share = 1.0 / length

        @pl.loop(0, D // CHUNK)
        def _(c):
            cols = pl.ds(pl.multiple_of(c * CHUNK, CHUNK), CHUNK)
            scaled = batch_buf[:, cols].astype(F32) * share
            padded = jnp.concatenate([scaled, jnp.zeros((128 - ROWS, CHUNK), F32)], axis=0).astype(BF16)
            pooled = jnp.dot(member, padded, preferred_element_type=F32).astype(BF16)
            cot_all[:, :, :, :, cols] = pooled.reshape(NX, NY, NZ, TOK, CHUNK)

    hidden_t, gate_d, up_d = r["hidden_t"], r["gate_d"], r["up_d"]
    for half in range(2):
        contract(r["down_w"], cot_all, r["delta_t"], half, 0)

        @pl.loop(0, FF_HERE // FF_STEP)
        def _(i, half=half):
            rows = pl.ds(pl.multiple_of(i * FF_STEP, FF_STEP), FF_STEP)
            cols = pl.ds(half * SPAN, SPAN)
            gate, up, delta = r["gate_t"][rows, cols], r["up_t"][rows, cols], r["delta_t"][rows, :]
            sigmoid = jax.nn.sigmoid(gate)
            activation = gate * sigmoid
            hidden_t[rows, cols] = (activation * up).astype(BF16)
            up_d[rows, cols] = (delta * activation).astype(BF16)
            gate_d[rows, cols] = (delta * up * sigmoid * (1.0 + gate * (1.0 - sigmoid))).astype(BF16)

        here = pl.ds(half * SPAN, SPAN)
        r["gate_rows"][here, :] = gate_d[:, here].T
        r["up_rows"][here, :] = up_d[:, here].T

    links = Links(r["ring_send"], r["ring_recv"])
    gain_links = Links(r["gain_send"], r["gain_recv"])
    part_all, gain_y, gain_x, gain_z = r["part_all"], r["gain_y"], r["gain_x"], r["gain_z"]

    def cols_of(q):
        return pl.ds(q * Q, Q)

    def partial(quarter):
        @pl.loop(0, Q // CHUNK)
        def _(i):
            at = pl.ds(pl.multiple_of(quarter * Q + i * CHUNK, CHUNK), CHUNK)
            delta = jnp.dot(r["gate_rows"][...], r["gate_w"][:, at], preferred_element_type=F32)
            delta = delta + jnp.dot(r["up_rows"][...], r["up_w"][:, at], preferred_element_type=F32)
            tokens = normed_all[:, :, :, :, at].reshape(TOKENS, CHUNK).astype(F32)
            gain_y[place.y, :, at] = jnp.sum(delta * tokens, axis=0, keepdims=True)
            part_all[:, :, :, :, at] = delta.astype(BF16).reshape(NX, NY, NZ, TOK, CHUNK)

    def weight_grad(out_ref, rows_ref, buf, first, last):
        @pl.loop(first, last)
        def _(i):
            at = pl.ds(pl.multiple_of(i * CHUNK, CHUNK), CHUNK)
            tokens = buf[:, :, :, :, at].reshape(TOKENS, CHUNK)
            out_ref[:, at] = jnp.dot(rows_ref[...], tokens, preferred_element_type=F32).astype(BF16)

    first0 = RingSum(
        place,
        links,
        "z",
        lambda at, q: part_all.at[:, :, at, :, cols_of(q)],
        r["far_z0"],
        r["near_z0"],
        lambda q: r["sum0"].at[:, :, :, cols_of(q)],
    )
    first1 = RingSum(
        place,
        links,
        "x",
        lambda at, q: part_all.at[at, :, :, :, cols_of(2 + q)],
        r["far_x1"],
        r["near_x1"],
        lambda q: r["sum1"].at[:, :, :, cols_of(q)],
    )
    second0 = RingSum(
        place,
        links,
        "x",
        lambda at, q: r["sum0"].at[at, :, :, cols_of(q)],
        r["far_x0"],
        r["near_x0"],
        lambda q: r["two0"].at[:, :, cols_of(q)],
    )
    second1 = RingSum(
        place,
        links,
        "z",
        lambda at, q: r["sum1"].at[:, at, :, cols_of(q)],
        r["far_z1"],
        r["near_z1"],
        lambda q: r["two1"].at[:, :, cols_of(q)],
    )

    partial(0)
    first0.start(0)
    partial(2)
    first1.start(0)
    partial(1)
    first0.start(1)
    partial(3)
    first1.start(1)
    gain_copy = gain_links.send(gain_y.at[place.y], gain_y.at[place.y], y_dev)
    weight_grad(r["gate_grads"], gate_d, normed_all, 0, 6)
    first0.relay(0)
    first1.relay(0)
    first0.relay(1)
    first1.relay(1)
    weight_grad(r["gate_grads"], gate_d, normed_all, 6, 8)
    gain_copy.wait_recv()
    gain_x[place.x] = gain_y[0] + gain_y[1]
    gain_copies = [gain_links.send(gain_x.at[place.x], gain_x.at[place.x], d) for d in x_dev[1:]]
    weight_grad(r["up_grads"], up_d, normed_all, 0, 8)

    for copy in qds:
        copy.wait_recv()
    query_dir = r["qd_own"][rows_at(a), :]
    for k in range(NA - 1):
        query_dir = query_dir + r["qd_land"][k].astype(F32)
    q_unit, q_inverse = unit_rows(r["query"][...], EPS_NORM, False)
    r["query_grads"][...] = unit_back(query_dir, q_unit, q_inverse).astype(BF16)

    @pl.when(place.z != 0)
    def _():
        for copy in pdz:
            copy.wait_recv()
        passage_end()


    for q in range(2):
        first0.end(q)
        second0.start(q)
        first1.end(q)
        second1.start(q)
    for copy in gain_copies:
        copy.wait_recv()
    gain_z[place.z] = (gain_x[0] + gain_x[1]) + (gain_x[2] + gain_x[3])
    gain_copies = [gain_links.send(gain_z.at[place.z], gain_z.at[place.z], d) for d in z_dev[1:]]
    weight_grad(r["down_grads"], hidden_t, cot_all, 0, 4)
    for q in range(2):
        second0.relay(q)
        second1.relay(q)
    weight_grad(r["down_grads"], hidden_t, cot_all, 4, 8)
    two0, two1, y_recv = r["two0"], r["two1"], r["y_recv"]
    second0.end(0)
    second0.end(1)
    y0 = links.send(two0.at[1 - place.y], y_recv.at[0], y_dev)
    second1.end(0)
    second1.end(1)
    y1 = links.send(two1.at[1 - place.y], y_recv.at[1], y_dev)
    unit, inverse = unit_rows(r["inputs"][...], EPS_RMS, True)
    for copy in gain_copies:
        copy.wait_recv()
    r["gain_grads"][...] = ((gain_z[0] + gain_z[1]) + (gain_z[2] + gain_z[3])) / r["gain"][...]

    y0.wait_recv()
    y1.wait_recv()
    delta = jnp.concatenate(
        [
            two0[place.y].astype(F32) + y_recv[0].astype(F32),
            two1[place.y].astype(F32) + y_recv[1].astype(F32),
        ],
        axis=1,
    )
    scaled = delta * r["gain"][...]
    mean = jnp.sum(scaled * unit, axis=-1, keepdims=True) / D
    own_cot = cot_all[place.x, place.y, place.z].astype(F32)
    r["input_grads"][...] = (own_cot + inverse * (scaled - unit * mean)).astype(BF16)

    g0.sent()
    pl.when(not_last)(g1.sent)
    for copy in pz + py + qs + os + ts + pdy + pdr + qds:
        copy.wait_send()
    for k in range(1, NZ):
        pl.when(z_at[k] != 0)(pdz[k - 1].wait_send)
        pl.when(place.z == k)(to_root[k - 1].wait_send)

    @pl.when(at_root)
    def _():
        for copy in z_copies:
            copy.wait_send()

    @pl.when(on_column)
    def _():
        for copy in x_copies:
            copy.wait_send()

    pl.when(is_last & (place.y == 0))(y_copy.wait_send)
    links.finish()
    gain_links.finish()


VMEM = pltpu.VMEM
HBM = pltpu.HBM
LOADED = ("gate_w", "up_w", "down_w")
INPUTS = (("packed", VMEM), ("small", VMEM), ("gain", VMEM)) + tuple((name + "_hbm", HBM) for name in LOADED)
OUTPUTS = (
    ("query_grads", (ROWS, D), BF16),
    ("passage_grads", (ROWS, D), BF16),
    ("input_grads", (TOK, D), BF16),
    ("gain_grads", (1, D), F32),
    ("gate_grads", (FF_HERE, D), BF16),
    ("up_grads", (FF_HERE, D), BF16),
    ("down_grads", (FF_HERE, D), BF16),
)


def scratch():
    dma = pltpu.SemaphoreType.DMA
    every = pltpu.VMEM((NX, NY, NZ, TOK, D), BF16)
    weight = pltpu.VMEM((FF_HERE, D), BF16)
    wide = pltpu.VMEM((FF_HERE, TOKENS), F32)
    low = pltpu.VMEM((FF_HERE, TOKENS), BF16)
    tall = pltpu.VMEM((TOKENS, FF_HERE), BF16)
    items = [
        ("normed_own", pltpu.VMEM((TOK, D), BF16)),
        ("normed_all", every),
        ("cot_all", every),
        ("part_all", every),
        ("gate_w", weight),
        ("up_w", weight),
        ("down_w", weight),
        ("gate_t", wide),
        ("up_t", wide),
        ("delta_t", pltpu.VMEM((FF_HERE, SPAN), F32)),
        ("hidden_t", low),
        ("gate_d", low),
        ("up_d", low),
        ("gate_rows", tall),
        ("up_rows", tall),
        ("q_all", pltpu.VMEM((NA * ROWS, D), BF16)),
        ("p_all", pltpu.VMEM((NB * ROWS, D), BF16)),
        ("off_all", pltpu.VMEM((NA, ROWS, 128), jnp.int32)),
        ("tot_all", pltpu.VMEM((NA, ROWS, 128), F32)),
        ("qd_own", pltpu.VMEM((NA * ROWS, D), F32)),
        ("qd_low", pltpu.VMEM((NA * ROWS, D), BF16)),
        ("qd_land", pltpu.VMEM((NA - 1, ROWS, D), BF16)),
        ("pd_own", pltpu.VMEM((NB * ROWS, D), F32)),
        ("pd_low", pltpu.VMEM((NB * ROWS, D), BF16)),
        ("pd_y", pltpu.VMEM((3, 32, D), BF16)),
        ("pd_z", pltpu.VMEM((3, ROWS, D), BF16)),
        ("batch_buf", pltpu.VMEM((ROWS, D), BF16)),
        ("far_z0", pltpu.VMEM((2, NX, NY, TOK, Q), BF16)),
        ("near_z0", pltpu.VMEM((2, 2, NX, NY, TOK, Q), BF16)),
        ("far_x0", pltpu.VMEM((2, NY, TOK, Q), BF16)),
        ("near_x0", pltpu.VMEM((2, 2, NY, TOK, Q), BF16)),
        ("far_x1", pltpu.VMEM((2, NY, NZ, TOK, Q), BF16)),
        ("near_x1", pltpu.VMEM((2, 2, NY, NZ, TOK, Q), BF16)),
        ("far_z1", pltpu.VMEM((2, NY, TOK, Q), BF16)),
        ("near_z1", pltpu.VMEM((2, 2, NY, TOK, Q), BF16)),
        ("sum0", pltpu.VMEM((NX, NY, TOK, H), BF16)),
        ("sum1", pltpu.VMEM((NY, NZ, TOK, H), BF16)),
        ("two0", pltpu.VMEM((NY, TOK, H), BF16)),
        ("two1", pltpu.VMEM((NY, TOK, H), BF16)),
        ("y_recv", pltpu.VMEM((2, TOK, H), BF16)),
        ("gain_y", pltpu.VMEM((2, 1, D), F32)),
        ("gain_x", pltpu.VMEM((4, 1, D), F32)),
        ("gain_z", pltpu.VMEM((4, 1, D), F32)),
        ("load_sem", dma((len(LOADED),))),
        ("g_send", dma((2, Gather.COPIES))),
        ("g_recv", dma((2, Gather.COPIES))),
        ("g_local", dma((2,))),
        ("b_send", dma((7,))),
        ("b_recv", dma((7,))),
        ("ring_send", dma((RING_COPIES,))),
        ("ring_recv", dma((RING_COPIES,))),
        ("gain_send", dma((7,))),
        ("gain_recv", dma((7,))),
    ]
    for name, count in (("pz", 4), ("py", 6), ("q", NA), ("o", NA), ("t", NA), ("pdy", 4), ("pdr", 4), ("root", 4), ("pdz", 4), ("qd", NA)):
        items += [(name + "_send", dma((count,))), (name + "_recv", dma((count,)))]
    return items


def write_kernel(*refs):
    count = len(OUTPUTS)
    copies = [pltpu.make_async_copy(refs[i], refs[count + i], refs[-1].at[i]) for i in reversed(range(count))]
    for copy in copies:
        copy.start()
    for copy in copies:
        copy.wait()


def local(
    query_cache,
    passage_cache,
    hard_offsets,
    passage_lengths,
    segment_inputs,
    segment_cotangents,
    norm_gain,
    gate_weight,
    up_weight,
    down_weight,
):
    packed = jnp.concatenate([query_cache, passage_cache, segment_inputs[0], segment_cotangents[0]], axis=0)
    small = jnp.concatenate([hard_offsets.reshape(1, ROWS), passage_lengths.reshape(1, ROWS)], axis=1)
    shapes = [jax.ShapeDtypeStruct(shape, kind) for _, shape, kind in OUTPUTS]
    results = pl.pallas_call(
        step_kernel,
        out_shape=shapes,
        in_specs=[pl.BlockSpec(memory_space=space) for _, space in INPUTS],
        out_specs=[pl.BlockSpec(memory_space=VMEM) for _ in OUTPUTS],
        scratch_shapes=[item for _, item in scratch()],
        compiler_params=pltpu.CompilerParams(
            collective_id=0, has_side_effects=True, vmem_limit_bytes=VMEM_LIMIT
        ),
        name="step",
    )(
        packed,
        small,
        norm_gain,
        gate_weight[0].T,
        up_weight[0].T,
        down_weight[0],
    )
    results = pl.pallas_call(
        write_kernel,
        out_shape=shapes,
        in_specs=[pl.BlockSpec(memory_space=VMEM) for _ in OUTPUTS],
        out_specs=[pl.BlockSpec(memory_space=HBM) for _ in OUTPUTS],
        scratch_shapes=[pltpu.SemaphoreType.DMA((len(OUTPUTS),))],
        compiler_params=pltpu.CompilerParams(vmem_limit_bytes=1024 * 1024),
        name="write",
    )(*results)
    query_grads, passage_grads, input_grads, gain_grads, gate_grads, up_grads, down_grads = results
    return (
        query_grads,
        passage_grads,
        input_grads[None],
        gate_grads.T[None],
        up_grads.T[None],
        down_grads[None],
        gain_grads,
    )


def solution(mesh):
    placed = (
        P(("dp", "segment"), None),
        P(("dp", "segment"), None),
        P(("dp", "segment"), None),
        P(),
        P("segment", "dp", None),
        P("segment", "dp", None),
        P("segment", None),
        P("segment", None, "dp"),
        P("segment", None, "dp"),
        P("segment", "dp", None),
    )
    return jax.shard_map(
        local,
        mesh=mesh,
        in_specs=placed,
        out_specs=(
            P(("dp", "segment"), None),
            P(("dp", "segment"), None),
            P("segment", "dp", None),
            P("segment", None, "dp"),
            P("segment", None, "dp"),
            P("segment", "dp", None),
            P("segment", None),
        ),
        check_vma=False,
    )
```

```python
import functools

import jax
import jax.numpy as jnp
from jax import lax
from jax.experimental import pallas as pl
from jax.experimental.pallas import tpu as pltpu
from jax.sharding import PartitionSpec as P

HN_BLOCK = 128
TAU = 0.02
PER_TAU = 1.0 / TAU
HN_WEIGHT = 64.0
EPS_NORM = 1e-06
EPS_RMS = 1e-05

D = 4096
ROWS = 8
TOK = 16
NX, NY, NZ = 4, 2, 4
NA, NB = 8, 16
H = D // 2
Q = D // 4
VMEM_LIMIT = 42 * 1024 * 1024
F32 = jnp.float32
BF16 = jnp.bfloat16
MESH = pl.DeviceIdType.MESH


class Place:
    def __init__(self):
        dp = lax.axis_index("dp")
        segment = lax.axis_index("segment")
        self.x = dp // 8
        self.y = lax.rem(dp // 4, 2)
        self.z = lax.rem(dp, 4)
        self.y_hi = segment // 2
        self.core = lax.rem(segment, 2)
        self.segment = segment

    def section(self, x=None, y=None, z=None):
        x = self.x if x is None else x
        y = self.y if y is None else y
        z = self.z if z is None else z
        return {"dp": x * 8 + y * 4 + z, "segment": self.segment}

    def shift(self, axis, by):
        at = getattr(self, axis)
        return lax.rem(at + by, 4)

    def a_index(self):
        return self.x * 2 + self.core

    def b_index(self):
        return (self.y_hi * 2 + self.y) * 4 + self.z

    def a_device(self, index):
        return {
            "dp": (index // 2) * 8 + self.y * 4 + self.z,
            "segment": self.y_hi * 2 + lax.rem(index, 2),
        }

    def b_device(self, index):
        y_all = index // 4
        return {
            "dp": self.x * 8 + lax.rem(y_all, 2) * 4 + lax.rem(index, 4),
            "segment": (y_all // 2) * 2 + self.core,
        }


def remote(src, dst, send_sem, recv_sem, device):
    return pltpu.make_async_remote_copy(
        src_ref=src, dst_ref=dst, send_sem=send_sem, recv_sem=recv_sem, device_id=device, device_id_type=MESH
    )


class Gather:
    COPIES = 25

    def __init__(self, place, src, buf, send_sem, recv_sem, local_sem):
        self.p, self.buf = place, buf
        self.send_sem, self.recv_sem = send_sem, recv_sem
        slot = buf.at[place.x, place.y, place.z]
        self.local = pltpu.make_async_copy(src, slot, local_sem)
        self.copies = {}
        self.add("y", src, slot, place.section(y=1 - place.y))
        for tag, axis, stage, base in (("a", "x", 0, 0), ("b", "z", 0, 2), ("c", "z", 1, 0), ("d", "x", 1, 2)):
            at = getattr(place, axis)
            left, right = place.shift(axis, 3), place.shift(axis, 1)
            plus, minus = place.section(**{axis: right}), place.section(**{axis: left})
            moves = (
                (at, base, plus),
                (at, base + 1, minus),
                (at, base + 1, plus),
                (at, base, minus),
                (left, base, plus),
                (right, base + 1, minus),
            )
            for k, (block, quarter, device) in enumerate(moves):
                view = self.view(axis, stage, block, quarter)
                self.add((tag, k), view, view, device)

    def add(self, key, src, dst, device):
        i = len(self.copies)
        self.copies[key] = remote(src, dst, self.send_sem.at[i], self.recv_sem.at[i], device)

    def view(self, axis, stage, at, quarter):
        p, c = self.p, pl.ds(quarter * Q, Q)
        if axis == "x":
            return self.buf.at[at, :, p.z, :, c] if stage == 0 else self.buf.at[at, :, :, :, c]
        return self.buf.at[p.x, :, at, :, c] if stage == 0 else self.buf.at[:, :, at, :, c]

    def begin(self, *keys):
        for key in keys:
            self.copies[key].start()

    def got(self, *keys):
        for key in keys:
            self.copies[key].wait_recv()

    def pair(self):
        self.local.start()
        self.begin("y")

    def small(self):
        self.local.wait()
        self.got("y")
        for k in range(4):
            self.begin(("a", k), ("b", k))

    def relay(self, one, two):
        for tag in (one, two):
            self.got((tag, 0))
            self.begin((tag, 4))
        for tag in (one, two):
            self.got((tag, 1))
            self.begin((tag, 5))

    def large_first(self):
        for tag in ("a", "b"):
            self.got(*[(tag, k) for k in (2, 3, 4, 5)])
        self.begin(("c", 0), ("d", 0), ("c", 1), ("d", 1))

    def large_second(self):
        self.begin(("c", 2), ("d", 2), ("c", 3), ("d", 3))

    def arrive(self):
        for tag in ("c", "d"):
            self.got(*[(tag, k) for k in (2, 3, 4, 5)])

    def sent(self):
        for copy in self.copies.values():
            copy.wait_send()


def unit_rows(values, eps, mean):
    widened = values.astype(F32)
    total = jnp.sum(widened * widened, axis=-1, keepdims=True)
    if mean:
        total = total / D
    inverse = lax.rsqrt(total + eps)
    return widened * inverse, inverse


def unit_back(gradient, unit_value, inverse):
    return inverse * (gradient - unit_value * jnp.sum(gradient * unit_value, axis=-1, keepdims=True))


def rows_at(index, rows=ROWS):
    return pl.ds(pl.multiple_of(index * rows, rows), rows)


class Links:
    def __init__(self, send_sem, recv_sem):
        self.send_sem, self.recv_sem = send_sem, recv_sem
        self.copies = []

    def send(self, src, dst, device):
        i = len(self.copies)
        copy = remote(src, dst, self.send_sem.at[i], self.recv_sem.at[i], device)
        copy.start()
        self.copies.append(copy)
        return copy

    def finish(self):
        for copy in self.copies:
            copy.wait_send()


class RingSum:
    def __init__(self, place, links, axis, part, far, near, out):
        self.p, self.links, self.axis = place, links, axis
        self.part, self.far, self.near, self.out = part, far, near, out
        self.plus = place.section(**{axis: place.shift(axis, 1)})
        self.minus = place.section(**{axis: place.shift(axis, 3)})
        self.at = [place.shift(axis, k) for k in range(4)]

    def start(self, q):
        send = self.links.send
        if q == 0:
            self.f0 = send(self.part(self.at[2], 0), self.far.at[0], self.plus)
            self.n10 = send(self.part(self.at[3], 0), self.near.at[1, 0], self.minus)
        else:
            self.f1 = send(self.part(self.at[2], 1), self.far.at[1], self.minus)
            self.n01 = send(self.part(self.at[1], 1), self.near.at[0, 1], self.plus)

    def relay(self, q):
        send = self.links.send
        if q == 0:
            self.f0.wait_recv()
            add_into(self.far.at[0], self.part(self.at[1], 0))
            self.n00 = send(self.far.at[0], self.near.at[0, 0], self.plus)
        else:
            self.f1.wait_recv()
            add_into(self.far.at[1], self.part(self.at[3], 1))
            self.n11 = send(self.far.at[1], self.near.at[1, 1], self.minus)

    def end(self, q):
        for copy in (self.n10, self.n00) if q == 0 else (self.n01, self.n11):
            copy.wait_recv()
        add_three(self.out(q), self.part(self.at[0], q), self.near.at[0, q], self.near.at[1, q])


def lead_loop(ref, body):
    shape = ref.shape
    lead = shape[:-2]
    count = 1
    for n in lead:
        count *= n

    @pl.loop(0, count)
    def _(i):
        index = []
        for n in reversed(lead):
            index.append(lax.rem(i, n))
            i = i // n
        body(tuple(reversed(index)))


def add_into(target, term):
    def body(i):
        target[i] = (target[i].astype(F32) + term[i].astype(F32)).astype(BF16)

    lead_loop(target, body)


def add_three(out, one, two, three):
    def body(i):
        out[i] = (one[i].astype(F32) + (two[i].astype(F32) + three[i].astype(F32))).astype(BF16)

    lead_loop(out, body)


TOKENS = NX * NY * NZ * TOK
SPAN = TOKENS // 2
CHUNK = 512
DEPTH = 1024
FF_HERE = 448
FF_STEP = 64
SLAB = NZ * TOK
RING_COPIES = 26


def step_kernel(*refs):
    names = [n for n, _ in INPUTS] + [n for n, _, _ in OUTPUTS] + [n for n, _ in scratch()]
    r = dict(zip(names, refs, strict=True))
    place = Place()
    a, b = place.a_index(), place.b_index()
    y_all = place.y_hi * 2 + place.y
    a_at = [lax.rem(a + k, NA) for k in range(NA)]
    a_dev = [place.a_device(i) for i in a_at]
    z_at = [place.shift("z", k) for k in range(NZ)]
    ya_at = [lax.rem(y_all + k, 4) for k in range(4)]
    z_dev = [place.section(z=z) for z in z_at]
    x_dev = [place.section(x=place.shift("x", k)) for k in range(NX)]
    ya_dev = [place.b_device(y * 4 + place.z) for y in ya_at]
    y_dev = place.section(y=1 - place.y)
    is_last = place.segment == 3
    not_last = jnp.logical_not(is_last)

    barrier = pltpu.get_barrier_semaphore()
    for device in a_dev[1:] + z_dev[1:] + ya_dev[1:]:
        pl.semaphore_signal(barrier, inc=1, device_id=device, device_id_type=MESH)

    loads = [
        pltpu.make_async_copy(r[name + "_hbm"], r[name], r["load_sem"].at[i])
        for i, name in enumerate(("gate_w", "up_w"))
    ]
    for i in range(FF_HERE // SLAB):
        slab = r["part_all"].at[i // NY, i % NY]
        loads.append(pltpu.make_async_copy(r["down_w_hbm"].at[i], slab, r["load_sem"].at[2 + i]))
    for copy in loads:
        copy.start()
    packed = r["packed"]
    r["query"] = packed.at[0:8]
    r["passage"] = packed.at[8:16]
    r["inputs"] = packed.at[16:32]
    r["cotangent"] = packed.at[32:48]

    def row_to_column(values):
        return jnp.sum(jnp.where(diagonal, jnp.broadcast_to(values, (ROWS, ROWS)), 0.0), axis=1, keepdims=True)

    lane = lax.broadcasted_iota(jnp.int32, (ROWS, ROWS), 1)
    diagonal = lane == lax.broadcasted_iota(jnp.int32, (ROWS, ROWS), 0)

    p_unit, _ = unit_rows(r["passage"][...], EPS_NORM, False)
    r["p_all"][rows_at(b), :] = p_unit.astype(BF16)
    q_unit, _ = unit_rows(r["query"][...], EPS_NORM, False)
    r["q_all"][rows_at(a), :] = q_unit.astype(BF16)
    normed, _ = unit_rows(r["inputs"][...], EPS_RMS, True)
    r["normed_own"][...] = (normed * r["gain"][...]).astype(BF16)
    column = row_to_column(r["small"][:, 0:8].astype(F32))
    r["off_all"][a] = jnp.broadcast_to(column, (ROWS, 128)).astype(jnp.int32)

    pl.semaphore_wait(barrier, NA + 5)

    def fan(devices, view_of, name):
        copies = []
        for k in range(1, len(devices)):
            src, dst = view_of(k)
            copy = remote(src, dst, r[name + "_send"].at[k], r[name + "_recv"].at[k], devices[k])
            copy.start()
            copies.append(copy)
        return copies

    normed_all, cot_all = r["normed_all"], r["cot_all"]
    g0 = Gather(place, r["normed_own"], normed_all, r["g_send"].at[0], r["g_recv"].at[0], r["g_local"].at[0])
    g1 = Gather(place, r["cotangent"], cot_all, r["g_send"].at[1], r["g_recv"].at[1], r["g_local"].at[1])

    own_p = r["p_all"].at[rows_at(b)]
    own_q = r["q_all"].at[rows_at(a)]
    def group(y, half):
        return r["p_all"].at[rows_at(y, 32), pl.ds(half * H, H)]

    y_moves = (
        (ya_at[0], 0, ya_dev[1]),
        (ya_at[0], 1, ya_dev[3]),
        (ya_at[0], 1, ya_dev[1]),
        (ya_at[0], 0, ya_dev[3]),
        (ya_at[3], 0, ya_dev[1]),
        (ya_at[1], 1, ya_dev[3]),
    )
    py = [
        remote(group(y, half), group(y, half), r["py_send"].at[k], r["py_recv"].at[k], device)
        for k, (y, half, device) in enumerate(y_moves)
    ]
    pz = fan(z_dev, lambda k: (own_p, own_p), "pz")
    g0.pair()
    pl.when(not_last)(g1.pair)
    for copy in pz:
        copy.wait_recv()
    for copy in py[:4]:
        copy.start()
    g0.small()
    qx = [remote(own_q, own_q, r["q_send"].at[k], r["q_recv"].at[k], a_dev[2 * k]) for k in range(1, NX)]
    for copy in qx:
        copy.start()
    sibling = place.a_device(place.x * 2 + 1 - place.core)
    q_from = [r["q_all"].at[rows_at(place.shift("x", (4 - k) % 4) * 2 + place.core)] for k in range(NX)]
    qs = [remote(q, q, r["qs_send"].at[k], r["qs_recv"].at[k], sibling) for k, q in enumerate(q_from)]
    qs[0].start()
    os = fan(a_dev, lambda k: (r["off_all"].at[a], r["off_all"].at[a]), "o")
    pl.when(not_last)(g1.small)
    py[0].wait_recv()
    py[4].start()
    py[1].wait_recv()
    py[5].start()
    g0.relay("a", "b")
    pl.when(not_last)(lambda: g1.relay("a", "b"))
    g0.large_first()
    g0.large_second()
    for k in range(1, NX):
        qx[k - 1].wait_recv()
        qs[k].start()

    for copy in qs + os + py[2:]:
        copy.wait_recv()
    scores = (
        lax.dot_general(r["q_all"][...], r["p_all"][...], (((1,), (1,)), ((), ())), preferred_element_type=F32)
        * PER_TAU
    )
    row = lax.broadcasted_iota(jnp.int32, (NA * ROWS, NB * ROWS), 0)
    col = lax.broadcasted_iota(jnp.int32, (NA * ROWS, NB * ROWS), 1)
    row_a, col_b = row >> 3, col >> 3
    row_dev = ((row_a >> 1) * 8 + place.y * 4 + place.z) * 4 + place.y_hi * 2 + (row_a & 1)
    row_index = row_dev * ROWS + (row & 7)
    col_y = col_b >> 2
    col_dev = (place.x * 8 + (col_y & 1) * 4 + (col_b & 3)) * 4 + (col_y >> 1) * 2 + place.core
    col_index = col_dev * ROWS + (col & 7)
    offsets = r["off_all"][...].reshape(NA * ROWS, 128)
    picked = (row_index >> 7) * HN_BLOCK + offsets
    weights = 1.0 + HN_WEIGHT * (picked == col_index).astype(F32)
    weighted = weights * jnp.exp(scores)
    part = jnp.sum(weighted, axis=1, keepdims=True)
    tot_all = r["tot_all"]
    on_row = col == row
    tot_all[a] = jnp.broadcast_to(jnp.sum(jnp.where(on_row, part, 0.0), axis=0, keepdims=True), (ROWS, 128))
    ts = fan(a_dev, lambda k: (tot_all.at[a], tot_all.at[a]), "t")
    g0.relay("c", "d")
    pl.when(not_last)(g1.large_first)

    for copy in ts:
        copy.wait_recv()
    totals = tot_all[0]
    for k in range(1, NA):
        totals = totals + tot_all[k]
    totals = jnp.broadcast_to(totals[:1, :], (NA * ROWS, 128))
    totals = jnp.sum(jnp.where(on_row, totals, 0.0), axis=1, keepdims=True)
    positive = (row_index == col_index).astype(F32)
    dscore = weighted / totals - positive
    dscore_low = dscore.astype(BF16)
    dscore_t = dscore.T.astype(BF16)

    def direction(left, right, own, low):
        @pl.loop(0, D // CHUNK)
        def _(c):
            cols = pl.ds(pl.multiple_of(c * CHUNK, CHUNK), CHUNK)
            value = jnp.dot(left, right[:, cols], preferred_element_type=F32) * PER_TAU
            own[:, cols] = value
            low[:, cols] = value.astype(BF16)

    pd_own, pd_low, pd_y, pd_z = r["pd_own"], r["pd_low"], r["pd_y"], r["pd_z"]
    direction(dscore_t, r["q_all"], pd_own, pd_low)
    head = pl.ds(0, ROWS)
    rest = pl.ds(ROWS, 3 * ROWS)

    def rest_of(y):
        return pl.ds(pl.multiple_of(y * 32 + ROWS, ROWS), 3 * ROWS)

    pdy = fan(ya_dev, lambda k: (pd_low.at[rows_at(ya_at[k] * 4)], pd_y.at[k - 1, head]), "pdy")
    pdr = fan(ya_dev, lambda k: (pd_low.at[rest_of(ya_at[k])], pd_y.at[k - 1, rest]), "pdr")
    direction(dscore_low, r["p_all"], r["qd_own"], r["qd_low"])
    pl.when(not_last)(g1.large_second)

    def gathered_rows(rows, local_rows, step):
        @pl.loop(0, D // step)
        def _(c):
            cols = pl.ds(pl.multiple_of(c * step, step), step)
            value = pd_own[rows, cols]
            for k in range(3):
                value = value + pd_y[k, local_rows, cols].astype(F32)
            pd_own[rows, cols] = value
            pd_low[rows, cols] = value.astype(BF16)

    for copy in pdy:
        copy.wait_recv()
    first_rows = rows_at(y_all * 4)
    gathered_rows(first_rows, head, 2 * DEPTH)
    root_dev = place.section(z=0)
    to_root = [
        remote(pd_low.at[first_rows], pd_z.at[k - 1], r["root_send"].at[k], r["root_recv"].at[k], root_dev)
        for k in range(1, NZ)
    ]
    for k in range(1, NZ):
        pl.when(place.z == k)(to_root[k - 1].start)
    pl.when(not_last)(lambda: g1.relay("c", "d"))

    g0.arrive()
    for copy in loads:
        copy.wait()

    def tokens_of(buf, half, at):
        return buf[2 * half : 2 * half + 2, :, :, :, at].reshape(SPAN, DEPTH)

    def contract(weight, buf, out, half, first):
        cols = pl.ds(first, SPAN)

        def one(i):
            at = pl.ds(pl.multiple_of(i * DEPTH, DEPTH), DEPTH)
            return lax.dot_general(
                weight[:, at], tokens_of(buf, half, at), (((1,), (1,)), ((), ())), preferred_element_type=F32
            )

        out[:, cols] = one(0)

        @pl.loop(1, D // DEPTH)
        def _(i):
            out[:, cols] += one(i)

    def delta_of(half):
        down, out = r["part_all"], r["delta_t"]
        upper, lower = pl.ds(0, 6 * SLAB), pl.ds(6 * SLAB, SLAB)

        def both(i):
            at = pl.ds(pl.multiple_of(i * DEPTH, DEPTH), DEPTH)
            tokens = tokens_of(cot_all, half, at)
            dims = (((1,), (1,)), ((), ()))
            one = down[0:3, :, :, :, at].reshape(6 * SLAB, DEPTH)
            two = down[3, 0, :, :, at].reshape(SLAB, DEPTH)
            return (
                lax.dot_general(one, tokens, dims, preferred_element_type=F32),
                lax.dot_general(two, tokens, dims, preferred_element_type=F32),
            )

        out[upper, :], out[lower, :] = both(0)

        @pl.loop(1, D // DEPTH)
        def _(i):
            one, two = both(i)
            out[upper, :] += one
            out[lower, :] += two

    contract(r["gate_w"], normed_all, r["gate_t"], 0, 0)

    def passage_end():
        passage_dir = pd_own[rows_at(b), :]
        for k in range(3):
            passage_dir = passage_dir + pd_z[k].astype(F32)
        unit, inverse = unit_rows(r["passage"][...], EPS_NORM, False)
        r["passage_grads"][...] = unit_back(passage_dir, unit, inverse).astype(BF16)

    @pl.when(place.z == 0)
    def _():
        for copy in to_root:
            copy.wait_recv()
        passage_end()

    batch_buf = r["batch_buf"]
    at_root = is_last & (place.x == 0) & (place.y == 0) & (place.z == 0)
    on_column = is_last & (place.x == 0) & (place.y == 0)

    def tree(i, device):
        return remote(batch_buf, batch_buf, r["b_send"].at[i], r["b_recv"].at[i], device)

    z_copies = [tree(k - 1, z_dev[k]) for k in range(1, NZ)]
    x_copies = [tree(2 + k, x_dev[k]) for k in range(1, NX)]
    y_copy = tree(6, y_dev)

    @pl.when(at_root)
    def _():
        batch_buf[...] = r["passage_grads"][...]
        for copy in z_copies:
            copy.start()

    contract(r["gate_w"], normed_all, r["gate_t"], 1, SPAN)

    for k in range(1, NZ):
        pl.when(on_column & (place.z == k))(z_copies[k - 1].wait_recv)

    @pl.when(on_column)
    def _():
        for copy in x_copies:
            copy.start()

    contract(r["up_w"], normed_all, r["up_t"], 0, 0)

    for k in range(1, NX):
        pl.when(is_last & (place.x == k) & (place.y == 0))(x_copies[k - 1].wait_recv)
    pl.when(is_last & (place.y == 0))(y_copy.start)
    contract(r["up_w"], normed_all, r["up_t"], 1, SPAN)
    qds = fan(a_dev, lambda k: (r["qd_low"].at[rows_at(a_at[k])], r["qd_land"].at[k - 1]), "qd")
    hidden_t, gate_d, up_d = r["hidden_t"], r["gate_d"], r["up_d"]

    @pl.loop(0, FF_HERE // FF_STEP)
    def _(i):
        rows = pl.ds(pl.multiple_of(i * FF_STEP, FF_STEP), FF_STEP)
        for half in range(2):
            cols = pl.ds(half * SPAN, SPAN)
            gate, up = r["gate_t"][rows, cols], r["up_t"][rows, cols]
            sigmoid = jax.nn.sigmoid(gate)
            activation = gate * sigmoid
            hidden_t[rows, cols] = (activation * up).astype(BF16)
            r["up_t"][rows, cols] = activation
            r["gate_t"][rows, cols] = up * sigmoid * (1.0 + gate * (1.0 - sigmoid))

    for copy in pdr:
        copy.wait_recv()
    gathered_rows(rest_of(y_all), rest, CHUNK)
    pdz = [
        remote(
            pd_low.at[rows_at(y_all * 4 + z_at[k])],
            pd_z.at[k - 1],
            r["pdz_send"].at[k],
            r["pdz_recv"].at[k],
            z_dev[k],
        )
        for k in range(1, NZ)
    ]
    for k in range(1, NZ):
        pl.when(z_at[k] != 0)(pdz[k - 1].start)
    pl.when(is_last & (place.y == 1))(y_copy.wait_recv)
    pl.when(not_last)(g1.arrive)

    @pl.when(is_last)
    def _():
        length = row_to_column(r["small"][:, 8:16].astype(F32))
        upto = jnp.where(lane >= lax.broadcasted_iota(jnp.int32, (ROWS, ROWS), 0), length, 0.0)
        last = jnp.sum(upto, axis=0, keepdims=True).astype(jnp.int32) - 1
        first = last - r["small"][:, 8:16] + 1
        last = jnp.concatenate([last, jnp.full((1, 128 - ROWS), -1, jnp.int32)], axis=1)
        first = jnp.concatenate([first, jnp.zeros((1, 128 - ROWS), jnp.int32)], axis=1)
        token = lax.broadcasted_iota(jnp.int32, (TOKENS, 128), 0)
        member = jnp.where((token >= first) & (token <= last), 1.0, 0.0).astype(BF16)
        share = 1.0 / length

        @pl.loop(0, D // CHUNK)
        def _(c):
            cols = pl.ds(pl.multiple_of(c * CHUNK, CHUNK), CHUNK)
            scaled = batch_buf[:, cols].astype(F32) * share
            padded = jnp.concatenate([scaled, jnp.zeros((128 - ROWS, CHUNK), F32)], axis=0).astype(BF16)
            pooled = jnp.dot(member, padded, preferred_element_type=F32).astype(BF16)
            cot_all[:, :, :, :, cols] = pooled.reshape(NX, NY, NZ, TOK, CHUNK)

    for half in range(2):
        delta_of(half)

        @pl.loop(0, FF_HERE // FF_STEP)
        def _(i, half=half):
            rows = pl.ds(pl.multiple_of(i * FF_STEP, FF_STEP), FF_STEP)
            cols = pl.ds(half * SPAN, SPAN)
            delta = r["delta_t"][rows, :]
            up_d[rows, cols] = (delta * r["up_t"][rows, cols]).astype(BF16)
            gate_d[rows, cols] = (delta * r["gate_t"][rows, cols]).astype(BF16)

        here = pl.ds(half * SPAN, SPAN)
        r["gate_rows"][here, :] = gate_d[:, here].T
        r["up_rows"][here, :] = up_d[:, here].T

    links = Links(r["ring_send"], r["ring_recv"])
    gain_links = Links(r["gain_send"], r["gain_recv"])
    part_all, gain_y, gain_x, gain_z = r["part_all"], r["gain_y"], r["gain_x"], r["gain_z"]

    def cols_of(q):
        return pl.ds(q * Q, Q)

    def partial(quarter):
        @pl.loop(0, Q // CHUNK)
        def _(i):
            at = pl.ds(pl.multiple_of(quarter * Q + i * CHUNK, CHUNK), CHUNK)
            delta = jnp.dot(r["gate_rows"][...], r["gate_w"][:, at], preferred_element_type=F32)
            delta = delta + jnp.dot(r["up_rows"][...], r["up_w"][:, at], preferred_element_type=F32)
            tokens = normed_all[:, :, :, :, at].reshape(TOKENS, CHUNK).astype(F32)
            gain_y[place.y, :, at] = jnp.sum(delta * tokens, axis=0, keepdims=True)
            part_all[:, :, :, :, at] = delta.astype(BF16).reshape(NX, NY, NZ, TOK, CHUNK)

    def weight_grad(out_ref, rows_ref, buf, first, last):
        @pl.loop(first, last)
        def _(i):
            at = pl.ds(pl.multiple_of(i * CHUNK, CHUNK), CHUNK)
            tokens = buf[:, :, :, :, at].reshape(TOKENS, CHUNK)
            out_ref[:, at] = jnp.dot(rows_ref[...], tokens, preferred_element_type=F32).astype(BF16)

    first0 = RingSum(
        place,
        links,
        "z",
        lambda at, q: part_all.at[:, :, at, :, cols_of(q)],
        r["far_z0"],
        r["near_z0"],
        lambda q: r["sum0"].at[:, :, :, cols_of(q)],
    )
    first1 = RingSum(
        place,
        links,
        "x",
        lambda at, q: part_all.at[at, :, :, :, cols_of(2 + q)],
        r["far_x1"],
        r["near_x1"],
        lambda q: r["sum1"].at[:, :, :, cols_of(q)],
    )
    second0 = RingSum(
        place,
        links,
        "x",
        lambda at, q: r["sum0"].at[at, :, :, cols_of(q)],
        r["far_x0"],
        r["near_x0"],
        lambda q: r["two0"].at[:, :, cols_of(q)],
    )
    second1 = RingSum(
        place,
        links,
        "z",
        lambda at, q: r["sum1"].at[:, at, :, cols_of(q)],
        r["far_z1"],
        r["near_z1"],
        lambda q: r["two1"].at[:, :, cols_of(q)],
    )

    partial(0)
    first0.start(0)
    partial(2)
    first1.start(0)
    partial(1)
    first0.start(1)
    partial(3)
    first1.start(1)
    gain_copy = gain_links.send(gain_y.at[place.y], gain_y.at[place.y], y_dev)
    weight_grad(r["gate_grads"], gate_d, normed_all, 0, 6)
    first0.relay(0)
    first1.relay(0)
    first0.relay(1)
    first1.relay(1)
    weight_grad(r["gate_grads"], gate_d, normed_all, 6, 8)
    gain_copy.wait_recv()
    gain_x[place.x] = gain_y[0] + gain_y[1]
    gain_copies = [gain_links.send(gain_x.at[place.x], gain_x.at[place.x], d) for d in x_dev[1:]]
    weight_grad(r["up_grads"], up_d, normed_all, 0, 8)

    for copy in qds:
        copy.wait_recv()
    query_dir = r["qd_own"][rows_at(a), :]
    for k in range(NA - 1):
        query_dir = query_dir + r["qd_land"][k].astype(F32)
    q_unit, q_inverse = unit_rows(r["query"][...], EPS_NORM, False)
    r["query_grads"][...] = unit_back(query_dir, q_unit, q_inverse).astype(BF16)

    @pl.when(place.z != 0)
    def _():
        for copy in pdz:
            copy.wait_recv()
        passage_end()


    for q in range(2):
        first0.end(q)
        second0.start(q)
        first1.end(q)
        second1.start(q)
    for copy in gain_copies:
        copy.wait_recv()
    gain_z[place.z] = (gain_x[0] + gain_x[1]) + (gain_x[2] + gain_x[3])
    gain_copies = [gain_links.send(gain_z.at[place.z], gain_z.at[place.z], d) for d in z_dev[1:]]
    weight_grad(r["down_grads"], hidden_t, cot_all, 0, 4)
    for q in range(2):
        second0.relay(q)
        second1.relay(q)
    weight_grad(r["down_grads"], hidden_t, cot_all, 4, 8)
    two0, two1, y_recv = r["two0"], r["two1"], r["y_recv"]
    second0.end(0)
    second0.end(1)
    y0 = links.send(two0.at[1 - place.y], y_recv.at[0], y_dev)
    second1.end(0)
    second1.end(1)
    y1 = links.send(two1.at[1 - place.y], y_recv.at[1], y_dev)
    unit, inverse = unit_rows(r["inputs"][...], EPS_RMS, True)
    for copy in gain_copies:
        copy.wait_recv()
    r["gain_grads"][...] = ((gain_z[0] + gain_z[1]) + (gain_z[2] + gain_z[3])) / r["gain"][...]

    y0.wait_recv()
    y1.wait_recv()
    delta = jnp.concatenate(
        [
            two0[place.y].astype(F32) + y_recv[0].astype(F32),
            two1[place.y].astype(F32) + y_recv[1].astype(F32),
        ],
        axis=1,
    )
    scaled = delta * r["gain"][...]
    mean = jnp.sum(scaled * unit, axis=-1, keepdims=True) / D
    own_cot = cot_all[place.x, place.y, place.z].astype(F32)
    r["input_grads"][...] = (own_cot + inverse * (scaled - unit * mean)).astype(BF16)

    g0.sent()
    pl.when(not_last)(g1.sent)
    for copy in pz + py + qx + qs + os + ts + pdy + pdr + qds:
        copy.wait_send()
    for k in range(1, NZ):
        pl.when(z_at[k] != 0)(pdz[k - 1].wait_send)
        pl.when(place.z == k)(to_root[k - 1].wait_send)

    @pl.when(at_root)
    def _():
        for copy in z_copies:
            copy.wait_send()

    @pl.when(on_column)
    def _():
        for copy in x_copies:
            copy.wait_send()

    pl.when(is_last & (place.y == 0))(y_copy.wait_send)
    links.finish()
    gain_links.finish()


VMEM = pltpu.VMEM
HBM = pltpu.HBM
LOADED = ("gate_w", "up_w", "down_w")
INPUTS = (("packed", VMEM), ("small", VMEM), ("gain", VMEM)) + tuple((name + "_hbm", HBM) for name in LOADED)
OUTPUTS = (
    ("query_grads", (ROWS, D), BF16),
    ("passage_grads", (ROWS, D), BF16),
    ("input_grads", (TOK, D), BF16),
    ("gain_grads", (1, D), F32),
    ("gate_grads", (FF_HERE, D), BF16),
    ("up_grads", (FF_HERE, D), BF16),
    ("down_grads", (FF_HERE, D), BF16),
)


def scratch():
    dma = pltpu.SemaphoreType.DMA
    every = pltpu.VMEM((NX, NY, NZ, TOK, D), BF16)
    weight = pltpu.VMEM((FF_HERE, D), BF16)
    wide = pltpu.VMEM((FF_HERE, TOKENS), F32)
    low = pltpu.VMEM((FF_HERE, TOKENS), BF16)
    tall = pltpu.VMEM((TOKENS, FF_HERE), BF16)
    items = [
        ("normed_own", pltpu.VMEM((TOK, D), BF16)),
        ("normed_all", every),
        ("cot_all", every),
        ("part_all", every),
        ("gate_w", weight),
        ("up_w", weight),
        ("gate_t", wide),
        ("up_t", wide),
        ("delta_t", pltpu.VMEM((FF_HERE, SPAN), F32)),
        ("hidden_t", low),
        ("gate_d", low),
        ("up_d", low),
        ("gate_rows", tall),
        ("up_rows", tall),
        ("q_all", pltpu.VMEM((NA * ROWS, D), BF16)),
        ("p_all", pltpu.VMEM((NB * ROWS, D), BF16)),
        ("off_all", pltpu.VMEM((NA, ROWS, 128), jnp.int32)),
        ("tot_all", pltpu.VMEM((NA, ROWS, 128), F32)),
        ("qd_own", pltpu.VMEM((NA * ROWS, D), F32)),
        ("qd_low", pltpu.VMEM((NA * ROWS, D), BF16)),
        ("qd_land", pltpu.VMEM((NA - 1, ROWS, D), BF16)),
        ("pd_own", pltpu.VMEM((NB * ROWS, D), F32)),
        ("pd_low", pltpu.VMEM((NB * ROWS, D), BF16)),
        ("pd_y", pltpu.VMEM((3, 32, D), BF16)),
        ("pd_z", pltpu.VMEM((3, ROWS, D), BF16)),
        ("batch_buf", pltpu.VMEM((ROWS, D), BF16)),
        ("far_z0", pltpu.VMEM((2, NX, NY, TOK, Q), BF16)),
        ("near_z0", pltpu.VMEM((2, 2, NX, NY, TOK, Q), BF16)),
        ("far_x0", pltpu.VMEM((2, NY, TOK, Q), BF16)),
        ("near_x0", pltpu.VMEM((2, 2, NY, TOK, Q), BF16)),
        ("far_x1", pltpu.VMEM((2, NY, NZ, TOK, Q), BF16)),
        ("near_x1", pltpu.VMEM((2, 2, NY, NZ, TOK, Q), BF16)),
        ("far_z1", pltpu.VMEM((2, NY, TOK, Q), BF16)),
        ("near_z1", pltpu.VMEM((2, 2, NY, TOK, Q), BF16)),
        ("sum0", pltpu.VMEM((NX, NY, TOK, H), BF16)),
        ("sum1", pltpu.VMEM((NY, NZ, TOK, H), BF16)),
        ("two0", pltpu.VMEM((NY, TOK, H), BF16)),
        ("two1", pltpu.VMEM((NY, TOK, H), BF16)),
        ("y_recv", pltpu.VMEM((2, TOK, H), BF16)),
        ("gain_y", pltpu.VMEM((2, 1, D), F32)),
        ("gain_x", pltpu.VMEM((4, 1, D), F32)),
        ("gain_z", pltpu.VMEM((4, 1, D), F32)),
        ("load_sem", dma((2 + FF_HERE // SLAB,))),
        ("g_send", dma((2, Gather.COPIES))),
        ("g_recv", dma((2, Gather.COPIES))),
        ("g_local", dma((2,))),
        ("b_send", dma((7,))),
        ("b_recv", dma((7,))),
        ("ring_send", dma((RING_COPIES,))),
        ("ring_recv", dma((RING_COPIES,))),
        ("gain_send", dma((7,))),
        ("gain_recv", dma((7,))),
    ]
    for name, count in (("pz", 4), ("py", 6), ("q", 4), ("qs", 4), ("o", NA), ("t", NA), ("pdy", 4), ("pdr", 4), ("root", 4), ("pdz", 4), ("qd", NA)):
        items += [(name + "_send", dma((count,))), (name + "_recv", dma((count,)))]
    return items


def write_kernel(*refs):
    count = len(OUTPUTS)
    copies = [pltpu.make_async_copy(refs[i], refs[count + i], refs[-1].at[i]) for i in reversed(range(count))]
    for copy in copies:
        copy.start()
    for copy in copies:
        copy.wait()


def local(
    query_cache,
    passage_cache,
    hard_offsets,
    passage_lengths,
    segment_inputs,
    segment_cotangents,
    norm_gain,
    gate_weight,
    up_weight,
    down_weight,
):
    packed = jnp.concatenate([query_cache, passage_cache, segment_inputs[0], segment_cotangents[0]], axis=0)
    small = jnp.concatenate([hard_offsets.reshape(1, ROWS), passage_lengths.reshape(1, ROWS)], axis=1)
    shapes = [jax.ShapeDtypeStruct(shape, kind) for _, shape, kind in OUTPUTS]
    results = pl.pallas_call(
        step_kernel,
        out_shape=shapes,
        in_specs=[pl.BlockSpec(memory_space=space) for _, space in INPUTS],
        out_specs=[pl.BlockSpec(memory_space=VMEM) for _ in OUTPUTS],
        scratch_shapes=[item for _, item in scratch()],
        compiler_params=pltpu.CompilerParams(
            collective_id=0, has_side_effects=True, vmem_limit_bytes=VMEM_LIMIT
        ),
        name="step",
    )(
        packed,
        small,
        norm_gain,
        gate_weight[0].T,
        up_weight[0].T,
        down_weight[0].reshape(FF_HERE // SLAB, NZ, TOK, D),
    )
    results = pl.pallas_call(
        write_kernel,
        out_shape=shapes,
        in_specs=[pl.BlockSpec(memory_space=VMEM) for _ in OUTPUTS],
        out_specs=[pl.BlockSpec(memory_space=HBM) for _ in OUTPUTS],
        scratch_shapes=[pltpu.SemaphoreType.DMA((len(OUTPUTS),))],
        compiler_params=pltpu.CompilerParams(vmem_limit_bytes=1024 * 1024),
        name="write",
    )(*results)
    query_grads, passage_grads, input_grads, gain_grads, gate_grads, up_grads, down_grads = results
    return (
        query_grads,
        passage_grads,
        input_grads[None],
        gate_grads.T[None],
        up_grads.T[None],
        down_grads[None],
        gain_grads,
    )


def solution(mesh):
    placed = (
        P(("dp", "segment"), None),
        P(("dp", "segment"), None),
        P(("dp", "segment"), None),
        P(),
        P("segment", "dp", None),
        P("segment", "dp", None),
        P("segment", None),
        P("segment", None, "dp"),
        P("segment", None, "dp"),
        P("segment", "dp", None),
    )
    return jax.shard_map(
        local,
        mesh=mesh,
        in_specs=placed,
        out_specs=(
            P(("dp", "segment"), None),
            P(("dp", "segment"), None),
            P("segment", "dp", None),
            P("segment", None, "dp"),
            P("segment", None, "dp"),
            P("segment", "dp", None),
            P("segment", None),
        ),
        check_vma=False,
    )
```

```python
import functools

import jax
import jax.numpy as jnp
from jax import lax
from jax.experimental import pallas as pl
from jax.experimental.pallas import tpu as pltpu
from jax.sharding import PartitionSpec as P

HN_BLOCK = 128
TAU = 0.02
PER_TAU = 1.0 / TAU
HN_WEIGHT = 64.0
EPS_NORM = 1e-06
EPS_RMS = 1e-05

D = 4096
ROWS = 8
TOK = 16
NX, NY, NZ = 4, 2, 4
NA, NB = 8, 16
H = D // 2
Q = D // 4
VMEM_LIMIT = 42 * 1024 * 1024
F32 = jnp.float32
BF16 = jnp.bfloat16
MESH = pl.DeviceIdType.MESH


class Place:
    def __init__(self):
        dp = lax.axis_index("dp")
        segment = lax.axis_index("segment")
        self.x = dp // 8
        self.y = lax.rem(dp // 4, 2)
        self.z = lax.rem(dp, 4)
        self.y_hi = segment // 2
        self.core = lax.rem(segment, 2)
        self.segment = segment

    def section(self, x=None, y=None, z=None):
        x = self.x if x is None else x
        y = self.y if y is None else y
        z = self.z if z is None else z
        return {"dp": x * 8 + y * 4 + z, "segment": self.segment}

    def shift(self, axis, by):
        at = getattr(self, axis)
        return lax.rem(at + by, 4)

    def a_index(self):
        return self.x * 2 + self.core

    def b_index(self):
        return (self.y_hi * 2 + self.y) * 4 + self.z

    def a_device(self, index):
        return {
            "dp": (index // 2) * 8 + self.y * 4 + self.z,
            "segment": self.y_hi * 2 + lax.rem(index, 2),
        }

    def b_device(self, index):
        y_all = index // 4
        return {
            "dp": self.x * 8 + lax.rem(y_all, 2) * 4 + lax.rem(index, 4),
            "segment": (y_all // 2) * 2 + self.core,
        }


def remote(src, dst, send_sem, recv_sem, device):
    return pltpu.make_async_remote_copy(
        src_ref=src, dst_ref=dst, send_sem=send_sem, recv_sem=recv_sem, device_id=device, device_id_type=MESH
    )


class Gather:
    COPIES = 25

    def __init__(self, place, src, buf, send_sem, recv_sem, local_sem):
        self.p, self.buf = place, buf
        self.send_sem, self.recv_sem = send_sem, recv_sem
        slot = buf.at[place.x, place.y, place.z]
        self.local = pltpu.make_async_copy(src, slot, local_sem)
        self.copies = {}
        self.add("y", src, slot, place.section(y=1 - place.y))
        for tag, axis, stage, base in (("a", "x", 0, 0), ("b", "z", 0, 2), ("c", "z", 1, 0), ("d", "x", 1, 2)):
            at = getattr(place, axis)
            left, right = place.shift(axis, 3), place.shift(axis, 1)
            plus, minus = place.section(**{axis: right}), place.section(**{axis: left})
            moves = (
                (at, base, plus),
                (at, base + 1, minus),
                (at, base + 1, plus),
                (at, base, minus),
                (left, base, plus),
                (right, base + 1, minus),
            )
            for k, (block, quarter, device) in enumerate(moves):
                view = self.view(axis, stage, block, quarter)
                self.add((tag, k), view, view, device)

    def add(self, key, src, dst, device):
        i = len(self.copies)
        self.copies[key] = remote(src, dst, self.send_sem.at[i], self.recv_sem.at[i], device)

    def view(self, axis, stage, at, quarter):
        p, c = self.p, pl.ds(quarter * Q, Q)
        if axis == "x":
            return self.buf.at[at, :, p.z, :, c] if stage == 0 else self.buf.at[at, :, :, :, c]
        return self.buf.at[p.x, :, at, :, c] if stage == 0 else self.buf.at[:, :, at, :, c]

    def begin(self, *keys):
        for key in keys:
            self.copies[key].start()

    def got(self, *keys):
        for key in keys:
            self.copies[key].wait_recv()

    def pair(self):
        self.local.start()
        self.begin("y")

    def small(self):
        self.local.wait()
        self.got("y")
        for k in range(4):
            self.begin(("a", k), ("b", k))

    def relay(self, one, two):
        for tag in (one, two):
            self.got((tag, 0))
            self.begin((tag, 4))
        for tag in (one, two):
            self.got((tag, 1))
            self.begin((tag, 5))

    def large_first(self):
        for tag in ("a", "b"):
            self.got(*[(tag, k) for k in (2, 3, 4, 5)])
        self.begin(("c", 0), ("d", 0), ("c", 1), ("d", 1))

    def large_second(self):
        self.begin(("c", 2), ("d", 2), ("c", 3), ("d", 3))

    def arrive(self):
        for tag in ("c", "d"):
            self.got(*[(tag, k) for k in (2, 3, 4, 5)])

    def sent(self):
        for copy in self.copies.values():
            copy.wait_send()


def unit_rows(values, eps, mean):
    widened = values.astype(F32)
    total = jnp.sum(widened * widened, axis=-1, keepdims=True)
    if mean:
        total = total / D
    inverse = lax.rsqrt(total + eps)
    return widened * inverse, inverse


def unit_back(gradient, unit_value, inverse):
    return inverse * (gradient - unit_value * jnp.sum(gradient * unit_value, axis=-1, keepdims=True))


def rows_at(index, rows=ROWS):
    return pl.ds(pl.multiple_of(index * rows, rows), rows)


class Links:
    def __init__(self, send_sem, recv_sem):
        self.send_sem, self.recv_sem = send_sem, recv_sem
        self.copies = []

    def send(self, src, dst, device):
        i = len(self.copies)
        copy = remote(src, dst, self.send_sem.at[i], self.recv_sem.at[i], device)
        copy.start()
        self.copies.append(copy)
        return copy

    def finish(self):
        for copy in self.copies:
            copy.wait_send()


class RingSum:
    def __init__(self, place, links, axis, part, far, near, out):
        self.p, self.links, self.axis = place, links, axis
        self.part, self.far, self.near, self.out = part, far, near, out
        self.plus = place.section(**{axis: place.shift(axis, 1)})
        self.minus = place.section(**{axis: place.shift(axis, 3)})
        self.at = [place.shift(axis, k) for k in range(4)]

    def start(self, q):
        send = self.links.send
        if q == 0:
            self.f0 = send(self.part(self.at[2], 0), self.far.at[0], self.plus)
            self.n10 = send(self.part(self.at[3], 0), self.near.at[1, 0], self.minus)
        else:
            self.f1 = send(self.part(self.at[2], 1), self.far.at[1], self.minus)
            self.n01 = send(self.part(self.at[1], 1), self.near.at[0, 1], self.plus)

    def relay(self, q):
        send = self.links.send
        if q == 0:
            self.f0.wait_recv()
            add_into(self.far.at[0], self.part(self.at[1], 0))
            self.n00 = send(self.far.at[0], self.near.at[0, 0], self.plus)
        else:
            self.f1.wait_recv()
            add_into(self.far.at[1], self.part(self.at[3], 1))
            self.n11 = send(self.far.at[1], self.near.at[1, 1], self.minus)

    def end(self, q):
        for copy in (self.n10, self.n00) if q == 0 else (self.n01, self.n11):
            copy.wait_recv()
        add_three(self.out(q), self.part(self.at[0], q), self.near.at[0, q], self.near.at[1, q])


def lead_loop(ref, body):
    shape = ref.shape
    lead = shape[:-2]
    count = 1
    for n in lead:
        count *= n

    @pl.loop(0, count)
    def _(i):
        index = []
        for n in reversed(lead):
            index.append(lax.rem(i, n))
            i = i // n
        body(tuple(reversed(index)))


def add_into(target, term):
    def body(i):
        target[i] = (target[i].astype(F32) + term[i].astype(F32)).astype(BF16)

    lead_loop(target, body)


def add_three(out, one, two, three):
    def body(i):
        out[i] = (one[i].astype(F32) + (two[i].astype(F32) + three[i].astype(F32))).astype(BF16)

    lead_loop(out, body)


TOKENS = NX * NY * NZ * TOK
SPAN = TOKENS // 2
CHUNK = 512
DEPTH = 1024
FF_HERE = 448
FF_STEP = 64
SLAB = NZ * TOK
RING_COPIES = 26


def step_kernel(*refs):
    names = [n for n, _ in INPUTS] + [n for n, _, _ in OUTPUTS] + [n for n, _ in scratch()]
    r = dict(zip(names, refs, strict=True))
    place = Place()
    a, b = place.a_index(), place.b_index()
    y_all = place.y_hi * 2 + place.y
    a_at = [lax.rem(a + k, NA) for k in range(NA)]
    a_dev = [place.a_device(i) for i in a_at]
    z_at = [place.shift("z", k) for k in range(NZ)]
    ya_at = [lax.rem(y_all + k, 4) for k in range(4)]
    z_dev = [place.section(z=z) for z in z_at]
    x_dev = [place.section(x=place.shift("x", k)) for k in range(NX)]
    ya_dev = [place.b_device(y * 4 + place.z) for y in ya_at]
    y_dev = place.section(y=1 - place.y)
    is_last = place.segment == 3
    not_last = jnp.logical_not(is_last)

    barrier = pltpu.get_barrier_semaphore()
    for device in a_dev[1:] + z_dev[1:] + ya_dev[1:]:
        pl.semaphore_signal(barrier, inc=1, device_id=device, device_id_type=MESH)

    loads = [
        pltpu.make_async_copy(r[name + "_hbm"], r[name], r["load_sem"].at[i])
        for i, name in enumerate(("gate_w", "up_w"))
    ]
    for i in range(FF_HERE // SLAB):
        slab = r["part_all"].at[i // NY, i % NY]
        loads.append(pltpu.make_async_copy(r["down_w_hbm"].at[i], slab, r["load_sem"].at[2 + i]))
    for copy in loads:
        copy.start()
    packed = r["packed"]
    r["query"] = packed.at[0:8]
    r["passage"] = packed.at[8:16]
    r["inputs"] = packed.at[16:32]
    r["cotangent"] = packed.at[32:48]

    def row_to_column(values):
        return jnp.sum(jnp.where(diagonal, jnp.broadcast_to(values, (ROWS, ROWS)), 0.0), axis=1, keepdims=True)

    lane = lax.broadcasted_iota(jnp.int32, (ROWS, ROWS), 1)
    diagonal = lane == lax.broadcasted_iota(jnp.int32, (ROWS, ROWS), 0)

    p_unit, _ = unit_rows(r["passage"][...], EPS_NORM, False)
    r["p_all"][rows_at(b), :] = p_unit.astype(BF16)
    q_unit, _ = unit_rows(r["query"][...], EPS_NORM, False)
    r["q_all"][rows_at(a), :] = q_unit.astype(BF16)
    normed, _ = unit_rows(r["inputs"][...], EPS_RMS, True)
    r["normed_own"][...] = (normed * r["gain"][...]).astype(BF16)
    column = row_to_column(r["small"][:, 0:8].astype(F32))
    r["off_all"][a] = jnp.broadcast_to(column, (ROWS, 128)).astype(jnp.int32)

    pl.semaphore_wait(barrier, NA + 5)

    def fan(devices, view_of, name):
        copies = []
        for k in range(1, len(devices)):
            src, dst = view_of(k)
            copy = remote(src, dst, r[name + "_send"].at[k], r[name + "_recv"].at[k], devices[k])
            copy.start()
            copies.append(copy)
        return copies

    normed_all, cot_all = r["normed_all"], r["cot_all"]
    g0 = Gather(place, r["normed_own"], normed_all, r["g_send"].at[0], r["g_recv"].at[0], r["g_local"].at[0])
    g1 = Gather(place, r["cotangent"], cot_all, r["g_send"].at[1], r["g_recv"].at[1], r["g_local"].at[1])

    own_p = r["p_all"].at[rows_at(b)]
    own_q = r["q_all"].at[rows_at(a)]
    def group(y, half):
        return r["p_all"].at[rows_at(y, 32), pl.ds(half * H, H)]

    y_moves = (
        (ya_at[0], 0, ya_dev[1]),
        (ya_at[0], 1, ya_dev[3]),
        (ya_at[0], 1, ya_dev[1]),
        (ya_at[0], 0, ya_dev[3]),
        (ya_at[3], 0, ya_dev[1]),
        (ya_at[1], 1, ya_dev[3]),
    )
    py = [
        remote(group(y, half), group(y, half), r["py_send"].at[k], r["py_recv"].at[k], device)
        for k, (y, half, device) in enumerate(y_moves)
    ]
    pz = fan(z_dev, lambda k: (own_p, own_p), "pz")
    g0.pair()
    pl.when(not_last)(g1.pair)
    for copy in pz:
        copy.wait_recv()
    for copy in py[:4]:
        copy.start()
    g0.small()
    qx = [remote(own_q, own_q, r["q_send"].at[k], r["q_recv"].at[k], a_dev[2 * k]) for k in range(1, NX)]
    for copy in qx:
        copy.start()
    sibling = place.a_device(place.x * 2 + 1 - place.core)
    q_from = [r["q_all"].at[rows_at(place.shift("x", (4 - k) % 4) * 2 + place.core)] for k in range(NX)]
    qs = [remote(q, q, r["qs_send"].at[k], r["qs_recv"].at[k], sibling) for k, q in enumerate(q_from)]
    qs[0].start()
    os = fan(a_dev, lambda k: (r["off_all"].at[a], r["off_all"].at[a]), "o")
    pl.when(not_last)(g1.small)
    py[0].wait_recv()
    py[4].start()
    py[1].wait_recv()
    py[5].start()
    g0.relay("a", "b")
    pl.when(not_last)(lambda: g1.relay("a", "b"))
    g0.large_first()
    g0.large_second()
    for k in range(1, NX):
        qx[k - 1].wait_recv()
        qs[k].start()

    for copy in qs + os + py[2:]:
        copy.wait_recv()
    scores = (
        lax.dot_general(r["q_all"][...], r["p_all"][...], (((1,), (1,)), ((), ())), preferred_element_type=F32)
        * PER_TAU
    )
    row = lax.broadcasted_iota(jnp.int32, (NA * ROWS, NB * ROWS), 0)
    col = lax.broadcasted_iota(jnp.int32, (NA * ROWS, NB * ROWS), 1)
    row_a, col_b = row >> 3, col >> 3
    row_dev = ((row_a >> 1) * 8 + place.y * 4 + place.z) * 4 + place.y_hi * 2 + (row_a & 1)
    row_index = row_dev * ROWS + (row & 7)
    col_y = col_b >> 2
    col_dev = (place.x * 8 + (col_y & 1) * 4 + (col_b & 3)) * 4 + (col_y >> 1) * 2 + place.core
    col_index = col_dev * ROWS + (col & 7)
    offsets = r["off_all"][...].reshape(NA * ROWS, 128)
    picked = (row_index >> 7) * HN_BLOCK + offsets
    weights = 1.0 + HN_WEIGHT * (picked == col_index).astype(F32)
    weighted = weights * jnp.exp(scores)
    part = jnp.sum(weighted, axis=1, keepdims=True)
    tot_all = r["tot_all"]
    on_row = col == row
    tot_all[a] = jnp.broadcast_to(jnp.sum(jnp.where(on_row, part, 0.0), axis=0, keepdims=True), (ROWS, 128))
    ts = fan(a_dev, lambda k: (tot_all.at[a], tot_all.at[a]), "t")
    g0.relay("c", "d")
    pl.when(not_last)(g1.large_first)

    for copy in ts:
        copy.wait_recv()
    totals = tot_all[0]
    for k in range(1, NA):
        totals = totals + tot_all[k]
    totals = jnp.broadcast_to(totals[:1, :], (NA * ROWS, 128))
    totals = jnp.sum(jnp.where(on_row, totals, 0.0), axis=1, keepdims=True)
    positive = (row_index == col_index).astype(F32)
    dscore = weighted / totals - positive
    dscore_low = dscore.astype(BF16)
    turned = dscore.T

    def direction(left, right, own, low):
        @pl.loop(0, D // CHUNK)
        def _(c):
            cols = pl.ds(pl.multiple_of(c * CHUNK, CHUNK), CHUNK)
            value = jnp.dot(left, right[:, cols], preferred_element_type=F32) * PER_TAU
            own[:, cols] = value
            low[:, cols] = value.astype(BF16)

    pd_own, pd_low, pd_y, pd_z = r["pd_own"], r["pd_low"], r["pd_y"], r["pd_z"]

    def passage_direction(skip, rows):
        starts = [y * 32 + skip for y in range(4)]
        left = jnp.concatenate([turned[at : at + rows] for at in starts], axis=0).astype(BF16)

        @pl.loop(0, D // CHUNK)
        def _(c):
            cols = pl.ds(pl.multiple_of(c * CHUNK, CHUNK), CHUNK)
            value = jnp.dot(left, r["q_all"][:, cols], preferred_element_type=F32) * PER_TAU
            for i, at in enumerate(starts):
                piece = value[i * rows : (i + 1) * rows]
                pd_own[pl.ds(at, rows), cols] = piece
                pd_low[pl.ds(at, rows), cols] = piece.astype(BF16)

    passage_direction(0, ROWS)
    head = pl.ds(0, ROWS)
    rest = pl.ds(ROWS, 3 * ROWS)

    def rest_of(y):
        return pl.ds(pl.multiple_of(y * 32 + ROWS, ROWS), 3 * ROWS)

    pdy = fan(ya_dev, lambda k: (pd_low.at[rows_at(ya_at[k] * 4)], pd_y.at[k - 1, head]), "pdy")
    passage_direction(ROWS, 3 * ROWS)
    pdr = fan(ya_dev, lambda k: (pd_low.at[rest_of(ya_at[k])], pd_y.at[k - 1, rest]), "pdr")
    direction(dscore_low, r["p_all"], r["qd_own"], r["qd_low"])
    pl.when(not_last)(g1.large_second)

    def gathered_rows(rows, local_rows, step):
        @pl.loop(0, D // step)
        def _(c):
            cols = pl.ds(pl.multiple_of(c * step, step), step)
            value = pd_own[rows, cols]
            for k in range(3):
                value = value + pd_y[k, local_rows, cols].astype(F32)
            pd_own[rows, cols] = value
            pd_low[rows, cols] = value.astype(BF16)

    for copy in pdy:
        copy.wait_recv()
    first_rows = rows_at(y_all * 4)
    gathered_rows(first_rows, head, 2 * DEPTH)
    root_dev = place.section(z=0)
    to_root = [
        remote(pd_low.at[first_rows], pd_z.at[k - 1], r["root_send"].at[k], r["root_recv"].at[k], root_dev)
        for k in range(1, NZ)
    ]
    for k in range(1, NZ):
        pl.when(place.z == k)(to_root[k - 1].start)
    pl.when(not_last)(lambda: g1.relay("c", "d"))

    g0.arrive()
    for copy in loads:
        copy.wait()

    def tokens_of(buf, half, at):
        return buf[2 * half : 2 * half + 2, :, :, :, at].reshape(SPAN, DEPTH)

    def contract(weight, buf, out, half, first):
        cols = pl.ds(first, SPAN)

        def one(i):
            at = pl.ds(pl.multiple_of(i * DEPTH, DEPTH), DEPTH)
            return lax.dot_general(
                weight[:, at], tokens_of(buf, half, at), (((1,), (1,)), ((), ())), preferred_element_type=F32
            )

        out[:, cols] = one(0)

        @pl.loop(1, D // DEPTH)
        def _(i):
            out[:, cols] += one(i)

    def delta_of(half):
        down, out = r["part_all"], r["delta_t"]
        upper, lower = pl.ds(0, 6 * SLAB), pl.ds(6 * SLAB, SLAB)

        def both(i):
            at = pl.ds(pl.multiple_of(i * DEPTH, DEPTH), DEPTH)
            tokens = tokens_of(cot_all, half, at)
            dims = (((1,), (1,)), ((), ()))
            one = down[0:3, :, :, :, at].reshape(6 * SLAB, DEPTH)
            two = down[3, 0, :, :, at].reshape(SLAB, DEPTH)
            return (
                lax.dot_general(one, tokens, dims, preferred_element_type=F32),
                lax.dot_general(two, tokens, dims, preferred_element_type=F32),
            )

        out[upper, :], out[lower, :] = both(0)

        @pl.loop(1, D // DEPTH)
        def _(i):
            one, two = both(i)
            out[upper, :] += one
            out[lower, :] += two

    contract(r["gate_w"], normed_all, r["gate_t"], 0, 0)

    def passage_end():
        passage_dir = pd_own[rows_at(b), :]
        for k in range(3):
            passage_dir = passage_dir + pd_z[k].astype(F32)
        unit, inverse = unit_rows(r["passage"][...], EPS_NORM, False)
        r["passage_grads"][...] = unit_back(passage_dir, unit, inverse).astype(BF16)

    @pl.when(place.z == 0)
    def _():
        for copy in to_root:
            copy.wait_recv()
        passage_end()

    batch_buf = r["batch_buf"]
    at_root = is_last & (place.x == 0) & (place.y == 0) & (place.z == 0)
    on_column = is_last & (place.x == 0) & (place.y == 0)

    def tree(i, device):
        return remote(batch_buf, batch_buf, r["b_send"].at[i], r["b_recv"].at[i], device)

    z_copies = [tree(k - 1, z_dev[k]) for k in range(1, NZ)]
    x_copies = [tree(2 + k, x_dev[k]) for k in range(1, NX)]
    y_copy = tree(6, y_dev)

    @pl.when(at_root)
    def _():
        batch_buf[...] = r["passage_grads"][...]
        for copy in z_copies:
            copy.start()

    contract(r["gate_w"], normed_all, r["gate_t"], 1, SPAN)

    for k in range(1, NZ):
        pl.when(on_column & (place.z == k))(z_copies[k - 1].wait_recv)

    @pl.when(on_column)
    def _():
        for copy in x_copies:
            copy.start()

    contract(r["up_w"], normed_all, r["up_t"], 0, 0)

    for k in range(1, NX):
        pl.when(is_last & (place.x == k) & (place.y == 0))(x_copies[k - 1].wait_recv)
    pl.when(is_last & (place.y == 0))(y_copy.start)
    contract(r["up_w"], normed_all, r["up_t"], 1, SPAN)
    qds = fan(a_dev, lambda k: (r["qd_low"].at[rows_at(a_at[k])], r["qd_land"].at[k - 1]), "qd")
    hidden_t, gate_d, up_d = r["hidden_t"], r["gate_d"], r["up_d"]

    @pl.loop(0, FF_HERE // FF_STEP)
    def _(i):
        rows = pl.ds(pl.multiple_of(i * FF_STEP, FF_STEP), FF_STEP)
        for half in range(2):
            cols = pl.ds(half * SPAN, SPAN)
            gate, up = r["gate_t"][rows, cols], r["up_t"][rows, cols]
            sigmoid = jax.nn.sigmoid(gate)
            activation = gate * sigmoid
            hidden_t[rows, cols] = (activation * up).astype(BF16)
            r["up_t"][rows, cols] = activation
            r["gate_t"][rows, cols] = up * sigmoid * (1.0 + gate * (1.0 - sigmoid))

    for copy in pdr:
        copy.wait_recv()
    gathered_rows(rest_of(y_all), rest, CHUNK)
    pdz = [
        remote(
            pd_low.at[rows_at(y_all * 4 + z_at[k])],
            pd_z.at[k - 1],
            r["pdz_send"].at[k],
            r["pdz_recv"].at[k],
            z_dev[k],
        )
        for k in range(1, NZ)
    ]
    for k in range(1, NZ):
        pl.when(z_at[k] != 0)(pdz[k - 1].start)
    pl.when(is_last & (place.y == 1))(y_copy.wait_recv)
    pl.when(not_last)(g1.arrive)

    @pl.when(is_last)
    def _():
        length = row_to_column(r["small"][:, 8:16].astype(F32))
        upto = jnp.where(lane >= lax.broadcasted_iota(jnp.int32, (ROWS, ROWS), 0), length, 0.0)
        last = jnp.sum(upto, axis=0, keepdims=True).astype(jnp.int32) - 1
        first = last - r["small"][:, 8:16] + 1
        last = jnp.concatenate([last, jnp.full((1, 128 - ROWS), -1, jnp.int32)], axis=1)
        first = jnp.concatenate([first, jnp.zeros((1, 128 - ROWS), jnp.int32)], axis=1)
        token = lax.broadcasted_iota(jnp.int32, (TOKENS, 128), 0)
        member = jnp.where((token >= first) & (token <= last), 1.0, 0.0).astype(BF16)
        share = 1.0 / length

        @pl.loop(0, D // CHUNK)
        def _(c):
            cols = pl.ds(pl.multiple_of(c * CHUNK, CHUNK), CHUNK)
            scaled = batch_buf[:, cols].astype(F32) * share
            padded = jnp.concatenate([scaled, jnp.zeros((128 - ROWS, CHUNK), F32)], axis=0).astype(BF16)
            pooled = jnp.dot(member, padded, preferred_element_type=F32).astype(BF16)
            cot_all[:, :, :, :, cols] = pooled.reshape(NX, NY, NZ, TOK, CHUNK)

    for half in range(2):
        delta_of(half)

        @pl.loop(0, FF_HERE // FF_STEP)
        def _(i, half=half):
            rows = pl.ds(pl.multiple_of(i * FF_STEP, FF_STEP), FF_STEP)
            cols = pl.ds(half * SPAN, SPAN)
            delta = r["delta_t"][rows, :]
            up_d[rows, cols] = (delta * r["up_t"][rows, cols]).astype(BF16)
            gate_d[rows, cols] = (delta * r["gate_t"][rows, cols]).astype(BF16)

        here = pl.ds(half * SPAN, SPAN)
        r["gate_rows"][here, :] = gate_d[:, here].T
        r["up_rows"][here, :] = up_d[:, here].T

    links = Links(r["ring_send"], r["ring_recv"])
    gain_links = Links(r["gain_send"], r["gain_recv"])
    part_all, gain_y, gain_x, gain_z = r["part_all"], r["gain_y"], r["gain_x"], r["gain_z"]

    def cols_of(q):
        return pl.ds(q * Q, Q)

    def partial(quarter):
        @pl.loop(0, Q // CHUNK)
        def _(i):
            at = pl.ds(pl.multiple_of(quarter * Q + i * CHUNK, CHUNK), CHUNK)
            delta = jnp.dot(r["gate_rows"][...], r["gate_w"][:, at], preferred_element_type=F32)
            delta = delta + jnp.dot(r["up_rows"][...], r["up_w"][:, at], preferred_element_type=F32)
            tokens = normed_all[:, :, :, :, at].reshape(TOKENS, CHUNK).astype(F32)
            gain_y[place.y, :, at] = jnp.sum(delta * tokens, axis=0, keepdims=True)
            part_all[:, :, :, :, at] = delta.astype(BF16).reshape(NX, NY, NZ, TOK, CHUNK)

    def weight_grad(out_ref, rows_ref, buf, first, last):
        @pl.loop(first, last)
        def _(i):
            at = pl.ds(pl.multiple_of(i * CHUNK, CHUNK), CHUNK)
            tokens = buf[:, :, :, :, at].reshape(TOKENS, CHUNK)
            out_ref[:, at] = jnp.dot(rows_ref[...], tokens, preferred_element_type=F32).astype(BF16)

    first0 = RingSum(
        place,
        links,
        "z",
        lambda at, q: part_all.at[:, :, at, :, cols_of(q)],
        r["far_z0"],
        r["near_z0"],
        lambda q: r["sum0"].at[:, :, :, cols_of(q)],
    )
    first1 = RingSum(
        place,
        links,
        "x",
        lambda at, q: part_all.at[at, :, :, :, cols_of(2 + q)],
        r["far_x1"],
        r["near_x1"],
        lambda q: r["sum1"].at[:, :, :, cols_of(q)],
    )
    second0 = RingSum(
        place,
        links,
        "x",
        lambda at, q: r["sum0"].at[at, :, :, cols_of(q)],
        r["far_x0"],
        r["near_x0"],
        lambda q: r["two0"].at[:, :, cols_of(q)],
    )
    second1 = RingSum(
        place,
        links,
        "z",
        lambda at, q: r["sum1"].at[:, at, :, cols_of(q)],
        r["far_z1"],
        r["near_z1"],
        lambda q: r["two1"].at[:, :, cols_of(q)],
    )

    partial(0)
    first0.start(0)
    partial(2)
    first1.start(0)
    partial(1)
    first0.start(1)
    partial(3)
    first1.start(1)
    gain_copy = gain_links.send(gain_y.at[place.y], gain_y.at[place.y], y_dev)
    weight_grad(r["gate_grads"], gate_d, normed_all, 0, 6)
    first0.relay(0)
    first1.relay(0)
    first0.relay(1)
    first1.relay(1)
    weight_grad(r["gate_grads"], gate_d, normed_all, 6, 8)
    gain_copy.wait_recv()
    gain_x[place.x] = gain_y[0] + gain_y[1]
    gain_copies = [gain_links.send(gain_x.at[place.x], gain_x.at[place.x], d) for d in x_dev[1:]]
    weight_grad(r["up_grads"], up_d, normed_all, 0, 8)

    for copy in qds:
        copy.wait_recv()
    query_dir = r["qd_own"][rows_at(a), :]
    for k in range(NA - 1):
        query_dir = query_dir + r["qd_land"][k].astype(F32)
    q_unit, q_inverse = unit_rows(r["query"][...], EPS_NORM, False)
    r["query_grads"][...] = unit_back(query_dir, q_unit, q_inverse).astype(BF16)

    @pl.when(place.z != 0)
    def _():
        for copy in pdz:
            copy.wait_recv()
        passage_end()


    for q in range(2):
        first0.end(q)
        second0.start(q)
        first1.end(q)
        second1.start(q)
    for copy in gain_copies:
        copy.wait_recv()
    gain_z[place.z] = (gain_x[0] + gain_x[1]) + (gain_x[2] + gain_x[3])
    gain_copies = [gain_links.send(gain_z.at[place.z], gain_z.at[place.z], d) for d in z_dev[1:]]
    weight_grad(r["down_grads"], hidden_t, cot_all, 0, 4)
    for q in range(2):
        second0.relay(q)
        second1.relay(q)
    weight_grad(r["down_grads"], hidden_t, cot_all, 4, 8)
    two0, two1, y_recv = r["two0"], r["two1"], r["y_recv"]
    second0.end(0)
    second0.end(1)
    y0 = links.send(two0.at[1 - place.y], y_recv.at[0], y_dev)
    second1.end(0)
    second1.end(1)
    y1 = links.send(two1.at[1 - place.y], y_recv.at[1], y_dev)
    unit, inverse = unit_rows(r["inputs"][...], EPS_RMS, True)
    for copy in gain_copies:
        copy.wait_recv()
    r["gain_grads"][...] = ((gain_z[0] + gain_z[1]) + (gain_z[2] + gain_z[3])) / r["gain"][...]

    y0.wait_recv()
    y1.wait_recv()
    delta = jnp.concatenate(
        [
            two0[place.y].astype(F32) + y_recv[0].astype(F32),
            two1[place.y].astype(F32) + y_recv[1].astype(F32),
        ],
        axis=1,
    )
    scaled = delta * r["gain"][...]
    mean = jnp.sum(scaled * unit, axis=-1, keepdims=True) / D
    own_cot = cot_all[place.x, place.y, place.z].astype(F32)
    r["input_grads"][...] = (own_cot + inverse * (scaled - unit * mean)).astype(BF16)

    g0.sent()
    pl.when(not_last)(g1.sent)
    for copy in pz + py + qx + qs + os + ts + pdy + pdr + qds:
        copy.wait_send()
    for k in range(1, NZ):
        pl.when(z_at[k] != 0)(pdz[k - 1].wait_send)
        pl.when(place.z == k)(to_root[k - 1].wait_send)

    @pl.when(at_root)
    def _():
        for copy in z_copies:
            copy.wait_send()

    @pl.when(on_column)
    def _():
        for copy in x_copies:
            copy.wait_send()

    pl.when(is_last & (place.y == 0))(y_copy.wait_send)
    links.finish()
    gain_links.finish()


VMEM = pltpu.VMEM
HBM = pltpu.HBM
LOADED = ("gate_w", "up_w", "down_w")
INPUTS = (("packed", VMEM), ("small", VMEM), ("gain", VMEM)) + tuple((name + "_hbm", HBM) for name in LOADED)
OUTPUTS = (
    ("query_grads", (ROWS, D), BF16),
    ("passage_grads", (ROWS, D), BF16),
    ("input_grads", (TOK, D), BF16),
    ("gain_grads", (1, D), F32),
    ("gate_grads", (FF_HERE, D), BF16),
    ("up_grads", (FF_HERE, D), BF16),
    ("down_grads", (FF_HERE, D), BF16),
)


def scratch():
    dma = pltpu.SemaphoreType.DMA
    every = pltpu.VMEM((NX, NY, NZ, TOK, D), BF16)
    weight = pltpu.VMEM((FF_HERE, D), BF16)
    wide = pltpu.VMEM((FF_HERE, TOKENS), F32)
    low = pltpu.VMEM((FF_HERE, TOKENS), BF16)
    tall = pltpu.VMEM((TOKENS, FF_HERE), BF16)
    items = [
        ("normed_own", pltpu.VMEM((TOK, D), BF16)),
        ("normed_all", every),
        ("cot_all", every),
        ("part_all", every),
        ("gate_w", weight),
        ("up_w", weight),
        ("gate_t", wide),
        ("up_t", wide),
        ("delta_t", pltpu.VMEM((FF_HERE, SPAN), F32)),
        ("hidden_t", low),
        ("gate_d", low),
        ("up_d", low),
        ("gate_rows", tall),
        ("up_rows", tall),
        ("q_all", pltpu.VMEM((NA * ROWS, D), BF16)),
        ("p_all", pltpu.VMEM((NB * ROWS, D), BF16)),
        ("off_all", pltpu.VMEM((NA, ROWS, 128), jnp.int32)),
        ("tot_all", pltpu.VMEM((NA, ROWS, 128), F32)),
        ("qd_own", pltpu.VMEM((NA * ROWS, D), F32)),
        ("qd_low", pltpu.VMEM((NA * ROWS, D), BF16)),
        ("qd_land", pltpu.VMEM((NA - 1, ROWS, D), BF16)),
        ("pd_own", pltpu.VMEM((NB * ROWS, D), F32)),
        ("pd_low", pltpu.VMEM((NB * ROWS, D), BF16)),
        ("pd_y", pltpu.VMEM((3, 32, D), BF16)),
        ("pd_z", pltpu.VMEM((3, ROWS, D), BF16)),
        ("batch_buf", pltpu.VMEM((ROWS, D), BF16)),
        ("far_z0", pltpu.VMEM((2, NX, NY, TOK, Q), BF16)),
        ("near_z0", pltpu.VMEM((2, 2, NX, NY, TOK, Q), BF16)),
        ("far_x0", pltpu.VMEM((2, NY, TOK, Q), BF16)),
        ("near_x0", pltpu.VMEM((2, 2, NY, TOK, Q), BF16)),
        ("far_x1", pltpu.VMEM((2, NY, NZ, TOK, Q), BF16)),
        ("near_x1", pltpu.VMEM((2, 2, NY, NZ, TOK, Q), BF16)),
        ("far_z1", pltpu.VMEM((2, NY, TOK, Q), BF16)),
        ("near_z1", pltpu.VMEM((2, 2, NY, TOK, Q), BF16)),
        ("sum0", pltpu.VMEM((NX, NY, TOK, H), BF16)),
        ("sum1", pltpu.VMEM((NY, NZ, TOK, H), BF16)),
        ("two0", pltpu.VMEM((NY, TOK, H), BF16)),
        ("two1", pltpu.VMEM((NY, TOK, H), BF16)),
        ("y_recv", pltpu.VMEM((2, TOK, H), BF16)),
        ("gain_y", pltpu.VMEM((2, 1, D), F32)),
        ("gain_x", pltpu.VMEM((4, 1, D), F32)),
        ("gain_z", pltpu.VMEM((4, 1, D), F32)),
        ("load_sem", dma((2 + FF_HERE // SLAB,))),
        ("g_send", dma((2, Gather.COPIES))),
        ("g_recv", dma((2, Gather.COPIES))),
        ("g_local", dma((2,))),
        ("b_send", dma((7,))),
        ("b_recv", dma((7,))),
        ("ring_send", dma((RING_COPIES,))),
        ("ring_recv", dma((RING_COPIES,))),
        ("gain_send", dma((7,))),
        ("gain_recv", dma((7,))),
    ]
    for name, count in (("pz", 4), ("py", 6), ("q", 4), ("qs", 4), ("o", NA), ("t", NA), ("pdy", 4), ("pdr", 4), ("root", 4), ("pdz", 4), ("qd", NA)):
        items += [(name + "_send", dma((count,))), (name + "_recv", dma((count,)))]
    return items


def write_kernel(*refs):
    count = len(OUTPUTS)
    copies = [pltpu.make_async_copy(refs[i], refs[count + i], refs[-1].at[i]) for i in reversed(range(count))]
    for copy in copies:
        copy.start()
    for copy in copies:
        copy.wait()


def local(
    query_cache,
    passage_cache,
    hard_offsets,
    passage_lengths,
    segment_inputs,
    segment_cotangents,
    norm_gain,
    gate_weight,
    up_weight,
    down_weight,
):
    packed = jnp.concatenate([query_cache, passage_cache, segment_inputs[0], segment_cotangents[0]], axis=0)
    small = jnp.concatenate([hard_offsets.reshape(1, ROWS), passage_lengths.reshape(1, ROWS)], axis=1)
    shapes = [jax.ShapeDtypeStruct(shape, kind) for _, shape, kind in OUTPUTS]
    results = pl.pallas_call(
        step_kernel,
        out_shape=shapes,
        in_specs=[pl.BlockSpec(memory_space=space) for _, space in INPUTS],
        out_specs=[pl.BlockSpec(memory_space=VMEM) for _ in OUTPUTS],
        scratch_shapes=[item for _, item in scratch()],
        compiler_params=pltpu.CompilerParams(
            collective_id=0, has_side_effects=True, vmem_limit_bytes=VMEM_LIMIT
        ),
        name="step",
    )(
        packed,
        small,
        norm_gain,
        gate_weight[0].T,
        up_weight[0].T,
        down_weight[0].reshape(FF_HERE // SLAB, NZ, TOK, D),
    )
    results = pl.pallas_call(
        write_kernel,
        out_shape=shapes,
        in_specs=[pl.BlockSpec(memory_space=VMEM) for _ in OUTPUTS],
        out_specs=[pl.BlockSpec(memory_space=HBM) for _ in OUTPUTS],
        scratch_shapes=[pltpu.SemaphoreType.DMA((len(OUTPUTS),))],
        compiler_params=pltpu.CompilerParams(vmem_limit_bytes=1024 * 1024),
        name="write",
    )(*results)
    query_grads, passage_grads, input_grads, gain_grads, gate_grads, up_grads, down_grads = results
    return (
        query_grads,
        passage_grads,
        input_grads[None],
        gate_grads.T[None],
        up_grads.T[None],
        down_grads[None],
        gain_grads,
    )


def solution(mesh):
    placed = (
        P(("dp", "segment"), None),
        P(("dp", "segment"), None),
        P(("dp", "segment"), None),
        P(),
        P("segment", "dp", None),
        P("segment", "dp", None),
        P("segment", None),
        P("segment", None, "dp"),
        P("segment", None, "dp"),
        P("segment", "dp", None),
    )
    return jax.shard_map(
        local,
        mesh=mesh,
        in_specs=placed,
        out_specs=(
            P(("dp", "segment"), None),
            P(("dp", "segment"), None),
            P("segment", "dp", None),
            P("segment", None, "dp"),
            P("segment", None, "dp"),
            P("segment", "dp", None),
            P("segment", None),
        ),
        check_vma=False,
    )
```
